32 devices in a mesh: fsdp: 8 (over z, y), tp: 4 (over x, core).
Axes of the slice: x: 2, y: 2, z: 4, core: 2. Of those that a mesh axis runs over, the one named last changes fastest.
Arguments:
- inputs: bfloat16 [16, 736, 1152], P('fsdp', 'tp'), may hold values from -6 to 6
- cotangent: bfloat16 [16, 736, 1152], P('fsdp', 'tp'), may hold values from -6 to 6
- lengths: int32 [16], P('fsdp'), may hold values from 1 to 729, as said below
- ln1_gain: bfloat16 [1152], P('fsdp'), may hold values from 0.099609375 to 1.8984375
- ln1_bias: bfloat16 [1152], P('fsdp'), may hold values from -0.3125 to 0.3125
- q_weight: bfloat16 [1152, 1152], P('fsdp', 'tp'), may hold values from -0.1875 to 0.1875
- q_bias: bfloat16 [1152], P('tp'), may hold values from -3 to 3
- k_weight: bfloat16 [1152, 1152], P('fsdp', 'tp'), may hold values from -0.1875 to 0.1875
- v_weight: bfloat16 [1152, 1152], P('fsdp', 'tp'), may hold values from -0.1875 to 0.1875
- v_bias: bfloat16 [1152], P('tp'), may hold values from -0.1875 to 0.1875
- out_weight: bfloat16 [1152, 1152], P('tp', 'fsdp'), may hold values from -2.5 to 2.5
- out_bias: bfloat16 [1152], P('fsdp'), may hold values from -1.75 to 1.75
- ln2_gain: bfloat16 [1152], P('fsdp'), may hold values from 0.099609375 to 1.8984375
- ln2_bias: bfloat16 [1152], P('fsdp'), may hold values from -1.75 to 1.75
- up_weight: bfloat16 [1152, 4304], P('fsdp', 'tp'), may hold values from -0.1875 to 0.1875
- up_bias: bfloat16 [4304], P('tp'), may hold values from -1.75 to 1.75
- down_weight: bfloat16 [4304, 1152], P('tp', 'fsdp'), may hold values from -0.09375 to 0.09375
- down_bias: bfloat16 [1152], P('fsdp'), may hold values from -1.75 to 1.75
Outputs:
- layer_out: bfloat16 [16, 736, 1152], P('fsdp', 'tp')
- input_grad: float32 [16, 736, 1152], P('fsdp', 'tp')
- ln1_gain_grad: float32 [1152], P('fsdp')
- ln1_bias_grad: float32 [1152], P('fsdp')
- q_weight_grad: float32 [1152, 1152], P('fsdp', 'tp')
- q_bias_grad: float32 [1152], P('tp')
- k_weight_grad: float32 [1152, 1152], P('fsdp', 'tp')
- v_weight_grad: float32 [1152, 1152], P('fsdp', 'tp')
- v_bias_grad: float32 [1152], P('tp')
- out_weight_grad: float32 [1152, 1152], P('tp', 'fsdp')
- out_bias_grad: float32 [1152], P('fsdp')
- ln2_gain_grad: float32 [1152], P('fsdp')
- ln2_bias_grad: float32 [1152], P('fsdp')
- up_weight_grad: float32 [1152, 4304], P('fsdp', 'tp')
- up_bias_grad: float32 [4304], P('tp')
- down_weight_grad: float32 [4304, 1152], P('tp', 'fsdp')
- down_bias_grad: float32 [1152], P('fsdp')
The draws below stay inside these ranges and needn't reach their ends.
Inputs may be any that keep to these rules, and one draw needn't show every extreme that they name: `lengths`: each slot either holds one image of 729 tokens or is empty with length 1; exactly 11 slots hold images, which ones drawn from the seed.
All inputs are finite; a program needn't handle non-finite values.
Results may differ from the reference program's by a relative error of at most 0.013.
Values may be sent and summed in bfloat16 or wider, within the bound.
No kernel may reach another device: no remote copies, remote signals or barrier semaphores. Data moves between devices by JAX's collectives and lax.ppermute only.
A program may use at most 192 MiB of HBM per device.

```python
import jax
import jax.numpy as jnp
from jax import lax

D = 1152
H = 16
HD = 72
FF = 4304
PATCHES = 729
SEQ = 736
SLOTS = 16
IMAGES = 11


def draw_lengths(key, part):
    order = jax.random.permutation(key, SLOTS)
    return jnp.where(order < IMAGES, PATCHES, 1).astype(jnp.int32)


def shard_levels(stream_key, dims, shards, low, top_value):
    def one(dim, blocks):
        draws = jax.random.uniform(jax.random.fold_in(jax.random.fold_in(stream_key, 6), dim), (blocks,), jnp.float32, low / len(shards), top_value / len(shards))
        return jnp.repeat(jnp.exp(draws), dims[dim] // blocks).reshape((-1,) + (1,) * (len(dims) - dim - 1))

    gain = one(*shards[0])
    for cut in shards[1:]:
        gain = gain * one(*cut)
    return gain


def scatter_about(own_key, shape, scale, reach, pieces=(), kind=jnp.bfloat16):
    entries = jax.random.normal(own_key, shape, jnp.float32) * scale
    if len(pieces) > 0:
        entries = shard_levels(own_key, shape, pieces, -0.22, 0.18) * entries
    return jnp.clip(entries, min=-reach, max=reach).astype(kind)


def setup_inputs(seed: int = 0) -> dict:
    splits = jax.random.split(jax.random.key(seed), 19)
    inputs = scatter_about(splits[0], (SLOTS, SEQ, D), 1.0, 6.0, ((0, 8), (1, 4)))
    cotangent = scatter_about(splits[1], (SLOTS, SEQ, D), 1.0, 6.0, ((0, 8), (1, 4)))
    lengths = draw_lengths(jax.random.fold_in(splits[18], 71), 0)
    ln1_gain = jnp.clip(1.0 + 0.18 * jax.random.normal(splits[3], (D,), jnp.float32), 0.099609375, 1.8984375).astype(jnp.bfloat16)
    ln1_bias = scatter_about(splits[4], (D,), 0.05, 0.3125, ((0, 8),))
    q_weight = scatter_about(splits[5], (D, H * HD), D ** -0.5, 0.1875, ((0, 8), (1, 4)))
    q_bias = scatter_about(splits[6], (H * HD,), 0.5, 3.0, ((0, 4),))
    k_weight = scatter_about(splits[7], (D, H * HD), D ** -0.5, 0.1875, ((0, 8), (1, 4)))
    v_weight = scatter_about(splits[8], (D, H * HD), D ** -0.5, 0.1875, ((0, 8), (1, 4)))
    v_bias = scatter_about(splits[9], (H * HD,), 0.03, 0.1875, ((0, 4),))
    out_weight = scatter_about(splits[10], (H * HD, D), (max(1, H * HD * 4 // PATCHES)) ** -0.5, 2.5, ((0, 4), (1, 8)))
    out_bias = scatter_about(splits[11], (D,), 0.3, 1.75, ((0, 8),))
    ln2_gain = jnp.clip(1.0 + 0.18 * jax.random.normal(splits[12], (D,), jnp.float32), 0.099609375, 1.8984375).astype(jnp.bfloat16)
    ln2_bias = scatter_about(splits[13], (D,), 0.3, 1.75, ((0, 8),))
    up_weight = scatter_about(splits[14], (D, FF), D ** -0.5, 0.1875, ((0, 8), (1, 4)))
    up_bias = scatter_about(splits[15], (FF,), 0.3, 1.75, ((0, 4),))
    down_weight = scatter_about(splits[16], (FF, D), FF ** -0.5, 0.09375, ((0, 4), (1, 8)))
    down_bias = scatter_about(splits[17], (D,), 0.3, 1.75, ((0, 8),))
    return dict(inputs=inputs, cotangent=cotangent, lengths=lengths, ln1_gain=ln1_gain, ln1_bias=ln1_bias, q_weight=q_weight, q_bias=q_bias, k_weight=k_weight, v_weight=v_weight, v_bias=v_bias, out_weight=out_weight, out_bias=out_bias, ln2_gain=ln2_gain, ln2_bias=ln2_bias, up_weight=up_weight, up_bias=up_bias, down_weight=down_weight, down_bias=down_bias)


@jax.custom_vjp
def low(v):
    return lax.optimization_barrier(v.astype(jnp.bfloat16)).astype(jnp.float32)

@jax.custom_vjp
def low_back(v):
    return v

def low_keep(v):
    return (low(v), None)

def low_pass(kept, grad):
    return (grad,)

def back_keep(v):
    return (v, None)

def back_low(kept, grad):
    return (low(grad),)
low.defvjp(low_keep, low_pass)
low_back.defvjp(back_keep, back_low)
epsilon = 1e-06
negative_big = -1e+30

def product(left, right):
    return jnp.dot(left, right, precision=lax.Precision.HIGHEST)

def layer_norm(row_block, gain_vec, shift_vec):
    average = lax.optimization_barrier(jnp.mean(row_block, -1, keepdims=True))
    center = row_block - average
    variance = lax.optimization_barrier(jnp.mean(center * center, -1, keepdims=True))
    return center * lax.rsqrt(variance + epsilon) * gain_vec + shift_vec

def slot_forward(weights, slot_rows, length):
    ln1_gain, ln1_bias, q_weight, q_bias, k_weight, v_weight, v_bias, out_weight, out_bias, ln2_gain, ln2_bias, up_weight, up_bias, down_weight, down_bias = weights
    norm_one = low(layer_norm(slot_rows, ln1_gain, ln1_bias))
    queries = low(low_back(product(norm_one, q_weight) + q_bias)).reshape(SEQ, H, HD)
    keys_all = low(low_back(product(norm_one, k_weight))).reshape(SEQ, H, HD)
    values_all = low(low_back(product(norm_one, v_weight) + v_bias)).reshape(SEQ, H, HD)
    scores = jnp.einsum('qhd,khd->hqk', queries, keys_all, precision=lax.Precision.HIGHEST)
    scores = low_back(scores * HD ** (-0.5))
    key_valid = jnp.arange(SEQ, dtype=jnp.int32) < length
    scores = jnp.where(key_valid[None, None, :], scores, negative_big)
    soft_weights = jax.nn.softmax(scores, axis=-1)
    mixed_heads = jnp.einsum('hqk,khd->qhd', low(soft_weights), values_all, precision=lax.Precision.HIGHEST)
    mixed_heads = low(low_back(mixed_heads)).reshape(SEQ, H * HD)
    middle = slot_rows + low_back(product(mixed_heads, out_weight)) + out_bias
    norm_two = low(layer_norm(middle, ln2_gain, ln2_bias))
    hidden = low_back(product(norm_two, up_weight) + up_bias)
    active = low(jax.nn.gelu(hidden, approximate=True))
    return middle + low_back(product(active, down_weight)) + down_bias

def reference(inputs, cotangent, lengths, ln1_gain, ln1_bias, q_weight, q_bias, k_weight, v_weight, v_bias, out_weight, out_bias, ln2_gain, ln2_bias, up_weight, up_bias, down_weight, down_bias):
    params = (ln1_gain, ln1_bias, q_weight, q_bias, k_weight, v_weight, v_bias, out_weight, out_bias, ln2_gain, ln2_bias, up_weight, up_bias, down_weight, down_bias)
    params = tuple((array_in.astype(jnp.float32) for array_in in params))

    def whole(block_in, *weights):

        def one_slot(slot_pair):
            return slot_forward(weights, slot_pair[0], slot_pair[1])
        return lax.map(jax.checkpoint(one_slot), (block_in, lengths))
    layer_value, pullback = jax.vjp(whole, inputs.astype(jnp.float32), *params)
    row_valid = (jnp.arange(SEQ, dtype=jnp.int32)[None, :] < lengths[:, None]).astype(jnp.float32)
    gradients = pullback(cotangent.astype(jnp.float32) * row_valid[:, :, None])
    return (layer_value.astype(jnp.bfloat16), gradients[0], gradients[1], gradients[2], gradients[3], gradients[4], gradients[5], gradients[6], gradients[7], gradients[8], gradients[9], gradients[10], gradients[11], gradients[12], gradients[13], gradients[14], gradients[15])
```

```python
import jax
import jax.numpy as jnp
from jax import lax
from jax.sharding import PartitionSpec as P

HD = 72
EPS = 1e-06
NEG = -1e30
BF = jnp.bfloat16
F32 = jnp.float32


def normalize(rows):
    average = jnp.mean(rows, -1, keepdims=True)
    center = rows - average
    variance = jnp.mean(center * center, -1, keepdims=True)
    inverse = lax.rsqrt(variance + EPS)
    return center * inverse, inverse


def norm_back(hat, inverse, gain, grad):
    scaled = grad * gain
    first = jnp.mean(scaled, -1, keepdims=True)
    second = jnp.mean(scaled * hat, -1, keepdims=True)
    return inverse * (scaled - first - hat * second)


def gelu_pair(v):
    c = 0.7978845608028654
    t = jnp.tanh(c * (v + 0.044715 * v * v * v))
    value = 0.5 * v * (1.0 + t)
    slope = 0.5 * (1.0 + t) + 0.5 * v * (1.0 - t * t) * (c * (1.0 + 3.0 * 0.044715 * v * v))
    return value, slope


def dot_nn(a, b):
    return lax.dot_general(a, b, (((1,), (0,)), ((), ())), preferred_element_type=F32)


def dot_nt(a, b):
    return lax.dot_general(a, b, (((1,), (1,)), ((), ())), preferred_element_type=F32)


def dot_tn(a, b):
    return lax.dot_general(a, b, (((0,), (0,)), ((), ())), preferred_element_type=F32)


def local(
    inputs,
    cotangent,
    lengths,
    ln1_gain,
    ln1_bias,
    q_weight,
    q_bias,
    k_weight,
    v_weight,
    v_bias,
    out_weight,
    out_bias,
    ln2_gain,
    ln2_bias,
    up_weight,
    up_bias,
    down_weight,
    down_bias,
):
    tp = lax.axis_size("tp")
    fs = lax.axis_size("fsdp")
    ti = lax.axis_index("tp")
    fi = lax.axis_index("fsdp")
    slots, rows, width = inputs.shape
    seq = rows * tp
    hw = q_weight.shape[1]
    units = up_weight.shape[1]
    heads = hw // HD
    scale = HD ** (-0.5)

    def swap_tp(x, k):
        return lax.ppermute(x, "tp", [(i, i ^ k) for i in range(tp)])

    def swap_fs(x, k):
        return lax.ppermute(x, "fsdp", [(i, i ^ k) for i in range(fs)])

    def gather_blocks(a):
        far = swap_tp(a, 2)
        near = swap_tp(jnp.stack([a, far], 0), 1)
        return jnp.concatenate([a, near[0], far, near[1]], 0)

    def block(a, j):
        return a[j * rows : (j + 1) * rows]

    def pair_sum(partial):
        other = swap_tp(
            jnp.concatenate([block(partial, 1), block(partial, 3)], 0).astype(BF), 1
        )
        mine = jnp.concatenate([block(partial, 0), block(partial, 2)], 0)
        return mine + other.astype(F32)

    def full_sum(partial):
        chip = pair_sum(partial).astype(BF)
        turned = jnp.concatenate([block(chip, 1), block(chip, 0)], 0)
        return chip.astype(F32) + swap_tp(turned, 2).astype(F32)

    def own_sum(partial):
        chip = pair_sum(partial)
        return block(chip, 0) + swap_tp(block(chip, 1).astype(BF), 2).astype(F32)

    def spread(half):
        near = swap_tp(half, 1)
        return jnp.concatenate([block(half, 0), block(near, 0), block(half, 1), block(near, 1)], 0)

    x_full = [gather_blocks(inputs[s]) for s in range(slots)]
    c_full = [gather_blocks(cotangent[s]) for s in range(slots)]

    small = jnp.stack([ln1_gain, ln1_bias, out_bias, ln2_gain, ln2_bias, down_bias, ln1_gain, ln1_gain], 0)
    small = lax.all_gather(small, "fsdp", axis=0)
    small = small.transpose(1, 0, 2).reshape(8, width).astype(F32)
    g1, b1, bo, g2, b2, bd = (small[i] for i in range(6))
    w_attn = jnp.concatenate([q_weight, k_weight, v_weight, out_weight.T], 1)
    w_attn = lax.all_gather(w_attn, "fsdp", axis=0, tiled=True)
    w_qkv = w_attn[:, : 3 * hw]
    wo_t = w_attn[:, 3 * hw :]
    pad = (-units) % 128
    w_mlp = jnp.concatenate(
        [jnp.pad(up_weight, ((0, 0), (0, pad))), jnp.pad(down_weight.T, ((0, 0), (0, pad)))], 1
    )
    w_mlp = lax.all_gather(w_mlp, "fsdp", axis=0, tiled=True)
    w_up = w_mlp[:, :units]
    wd_t = w_mlp[:, units + pad : 2 * units + pad]

    qkv_shift = jnp.concatenate([q_bias, jnp.zeros_like(q_bias), v_bias], 0).astype(F32)
    up_shift = up_bias.astype(F32)
    place = (
        (jnp.arange(tp, dtype=jnp.int32)[:, None] ^ ti) * rows
        + jnp.arange(rows, dtype=jnp.int32)[None, :]
    ).reshape(seq)

    def split_heads(a):
        return a.reshape(seq, heads, HD)

    outs, grads_x = [], []
    g_attn = g_mlp = None
    wide = head_sums = unit_sums = None
    for s in range(slots):
        valid = place < lengths[s]
        x = x_full[s].astype(F32)
        hat1, _ = normalize(x)
        n1 = (hat1 * g1 + b1).astype(BF)
        qkv = (dot_nn(n1, w_qkv) + qkv_shift).astype(BF)
        q, k, v = (split_heads(qkv[:, i * hw : (i + 1) * hw]) for i in range(3))
        scores = jnp.einsum("qhd,khd->hqk", q, k, preferred_element_type=F32) * scale
        scores = jnp.where(valid[None, None, :], scores, NEG)
        top = jnp.max(scores, -1, keepdims=True)
        lse = top + jnp.log(jnp.sum(jnp.exp(scores - top), -1, keepdims=True))
        probs = jnp.exp(scores - lse)
        probs_low = probs.astype(BF)
        mixed = jnp.einsum("hqk,khd->qhd", probs_low, v, preferred_element_type=F32)
        mixed = mixed.astype(BF).reshape(seq, hw)
        attended = full_sum(dot_nt(mixed, wo_t))
        x_half = jnp.concatenate([block(x, 0), block(x, 2)], 0)
        middle = x_half + attended + bo
        hat2, inv2 = normalize(middle)
        n2 = spread((hat2 * g2 + b2).astype(BF))
        hidden = dot_nn(n2, w_up) + up_shift
        value, slope = gelu_pair(hidden)
        active = value.astype(BF)
        outs.append((block(middle, 0) + own_sum(dot_nt(active, wd_t)) + bd).astype(BF))
        go = jnp.where(valid[:, None], c_full[s], jnp.zeros((), BF))
        g_down = dot_tn(go, active)
        gh = (dot_nn(go, wd_t) * slope).astype(BF)
        g_up = dot_tn(n2, gh)
        gn2 = full_sum(dot_nt(gh, w_up))
        go_half = jnp.concatenate([block(go, 0), block(go, 2)], 0).astype(F32)
        gm = go_half + norm_back(hat2, inv2, g2, gn2)
        gml = spread(gm.astype(BF))
        g_out = dot_tn(gml, mixed)
        gmix = split_heads(dot_nn(gml, wo_t).astype(BF))
        gp = jnp.einsum("qhd,khd->hqk", gmix, v, preferred_element_type=F32)
        inner = jnp.sum(probs * gp, -1, keepdims=True)
        gs = (probs * (gp - inner)).astype(BF)
        gq = (jnp.einsum("hqk,khd->qhd", gs, k, preferred_element_type=F32) * scale).astype(BF)
        gk = (jnp.einsum("hqk,qhd->khd", gs, q, preferred_element_type=F32) * scale).astype(BF)
        gv = jnp.einsum("hqk,qhd->khd", probs_low, gmix, preferred_element_type=F32).astype(BF)
        gqkv = jnp.concatenate([a.reshape(seq, hw) for a in (gq, gk, gv)], 1)
        g_qkv = dot_tn(n1, gqkv)
        gn1 = own_sum(dot_nt(gqkv, w_qkv))
        hat_own, inv_own = normalize(block(x, 0))
        grads_x.append(block(gm, 0) + norm_back(hat_own, inv_own, g1, gn1))
        gn2_own, hat2_own = block(gn2, 0), block(hat2, 0)
        wide_s = jnp.stack(
            [
                jnp.sum(hat_own * gn1, 0),
                jnp.sum(gn1, 0),
                jnp.sum(block(gm, 0), 0),
                jnp.sum(hat2_own * gn2_own, 0),
                jnp.sum(gn2_own, 0),
                jnp.sum(block(go_half, 0), 0),
            ],
            0,
        )
        col = jnp.sum(gqkv.astype(F32), 0)
        hs = jnp.stack([col[:hw], col[2 * hw :]], 0)
        us = jnp.sum(gh.astype(F32), 0)
        ga = jnp.concatenate([g_qkv, g_out], 1)
        gmm = (g_up, g_down)
        if s == 0:
            g_attn, g_mlp, wide, head_sums, unit_sums = ga, gmm, wide_s, hs, us
        else:
            g_attn = g_attn + ga
            g_mlp = (g_mlp[0] + gmm[0], g_mlp[1] + gmm[1])
            wide = wide + wide_s
            head_sums = head_sums + hs
            unit_sums = unit_sums + us
    gm_pack = jnp.concatenate([jnp.pad(a.astype(BF), ((0, 0), (0, pad))) for a in g_mlp], 1)
    r_mlp = lax.psum_scatter(gm_pack, "fsdp", scatter_dimension=0, tiled=True).astype(F32)
    r_attn = lax.psum_scatter(g_attn.astype(BF), "fsdp", scatter_dimension=0, tiled=True).astype(F32)

    wide = wide + swap_tp(wide, 1)
    wide = wide + swap_tp(wide, 2)
    line = jnp.concatenate([wide.reshape(-1), head_sums.reshape(-1), unit_sums], 0)
    step = 1
    while step < fs:
        line = line + swap_fs(line, step)
        step *= 2
    wide = line[: 6 * width].reshape(6, width)
    shard = width // fs
    wide = lax.dynamic_slice_in_dim(wide, fi * shard, shard, 1)
    head_sums = line[6 * width : 6 * width + 2 * hw].reshape(2, hw)
    unit_sums = line[6 * width + 2 * hw :]
    return (
        jnp.stack(outs, 0),
        jnp.stack(grads_x, 0),
        wide[0],
        wide[1],
        r_attn[:, :hw],
        head_sums[0],
        r_attn[:, hw : 2 * hw],
        r_attn[:, 2 * hw : 3 * hw],
        head_sums[1],
        r_attn[:, 3 * hw :].T,
        wide[2],
        wide[3],
        wide[4],
        r_mlp[:, :units],
        unit_sums,
        r_mlp[:, units + pad : 2 * units + pad].T,
        wide[5],
    )


def solution(mesh):
    rowed = P("fsdp", "tp", None)
    wide = P("fsdp")
    cols = P("fsdp", "tp")
    turned = P("tp", "fsdp")
    part = P("tp")
    in_specs = (
        rowed, rowed, wide, wide, wide, cols, part, cols, cols, part, turned, wide,
        wide, wide, cols, part, turned, wide,
    )
    out_specs = (
        rowed, rowed, wide, wide, cols, part, cols, cols, part, turned, wide, wide, wide,
        cols, part, turned, wide,
    )
    return jax.shard_map(local, mesh=mesh, in_specs=in_specs, out_specs=out_specs, check_vma=False)
```

```python
import functools

import jax
import jax.numpy as jnp
from jax import lax
from jax.experimental import pallas as pl
from jax.experimental.pallas import tpu as pltpu
from jax.sharding import PartitionSpec as P

HD = 72
EPS = 1e-06
BF = jnp.bfloat16
F32 = jnp.float32
LOG2E = 1.4426950408889634
CHUNK = 16
VM = pl.BlockSpec(memory_space=pltpu.VMEM)
SM = pl.BlockSpec(memory_space=pltpu.SMEM)
HBM = pl.BlockSpec(memory_space=pl.ANY)


def dg(a, b, ca, cb):
    return lax.dot_general(a, b, (((ca,), (cb,)), ((), ())), preferred_element_type=F32)


def call(body, name, ins, specs, outs, scratch, flops, exps=0, limit=48):
    shapes = [jax.ShapeDtypeStruct(s, d) for s, d in outs]
    moved = sum(a.size * a.dtype.itemsize for a in ins)
    moved += sum(s.size * s.dtype.itemsize for s in shapes)
    return pl.pallas_call(
        body,
        out_shape=shapes,
        in_specs=specs,
        out_specs=[VM] * len(outs),
        scratch_shapes=scratch,
        compiler_params=pltpu.CompilerParams(vmem_limit_bytes=limit << 20),
        name=name,
        cost_estimate=pl.CostEstimate(
            flops=int(flops), bytes_accessed=int(moved), transcendentals=int(exps)
        ),
    )(*ins)


def normal(x):
    average = jnp.mean(x, -1, keepdims=True)
    center = x - average
    variance = jnp.mean(center * center, -1, keepdims=True)
    inverse = lax.rsqrt(variance + EPS)
    return center * inverse, inverse


def normal_back(hat, inverse, scaled):
    first = jnp.mean(scaled, -1, keepdims=True)
    second = jnp.mean(scaled * hat, -1, keepdims=True)
    return inverse * (scaled - first - hat * second)


def positions(sc_ref, rows, shape, dim):
    r = lax.broadcasted_iota(jnp.int32, shape, dim)
    ti = sc_ref[0]
    p0, p2, p1, p3 = ((ti ^ j) * rows for j in (0, 2, 1, 3))
    return jnp.where(
        r < 2 * rows,
        jnp.where(r < rows, r + p0, r + (p2 - rows)),
        jnp.where(r < 3 * rows, r + (p1 - 2 * rows), r + (p3 - 3 * rows)),
    )


def attn_kernel(heads, rows, slot, sc_ref, xo, xf, xno, xnf, vec_ref, shift_ref, w_ref,
                n1_ref, qkv_ref, mixed_ref, lse_ref, keep_ref, send_ref, s_ref, p_ref):
    seq = 4 * rows
    half = 2 * rows
    hw = heads * HD
    c = LOG2E * HD**-0.5
    gain, bias = vec_ref[0:1, :], vec_ref[1:2, :]
    for i, pair in enumerate(((xo, xf), (xno, xnf))):
        parts = [normal(ref[slot].astype(F32))[0] * gain + bias for ref in pair]
        n1 = jnp.concatenate(parts, 0).astype(BF)
        n1_ref[i * half : (i + 1) * half, :] = n1
        qkv_ref[i * half : (i + 1) * half, :] = (dg(n1, w_ref[...], 1, 0) + shift_ref[...]).astype(BF)
    lane = lax.broadcasted_iota(jnp.int32, (seq, 128), 1)
    pos = positions(sc_ref, rows, (seq, 128), 0)
    mask = jnp.where((lane == HD) & (pos >= sc_ref[1]), -1e30, 0.0).astype(BF)
    one = jnp.where(lane == HD, 1.0, 0.0).astype(BF)
    for h in range(heads):
        a = hw + HD * h
        qx = jnp.where(lane < HD, qkv_ref[:, a : a + 128], one)
        kx = jnp.where(lane < HD, qkv_ref[:, hw + a : hw + a + 128], mask)
        v = qkv_ref[:, 2 * hw + a : 2 * hw + a + HD]
        sl = h % 2
        s_ref[sl] = dg(kx, qx, 1, 1)
        m = s_ref[sl, 0:CHUNK, :]
        for r in range(CHUNK, seq, CHUNK):
            m = jnp.maximum(m, s_ref[sl, r : r + CHUNK, :])
        m = jnp.max(m, 0, keepdims=True) * c
        total = jnp.zeros((CHUNK, seq), F32)
        for r in range(0, seq, CHUNK):
            p = jnp.exp2(s_ref[sl, r : r + CHUNK, :] * c - m)
            total = total + p
            p_ref[sl, r : r + CHUNK, :] = p.astype(BF)
        total = jnp.sum(total, 0, keepdims=True)
        lse_ref[h : h + 1, :] = m + jnp.log2(total)
        mixed = dg(v, p_ref[sl], 0, 0) * (1.0 / total)
        mixed_ref[:, HD * h : HD * h + HD] = mixed.T.astype(BF)
    for i, ref in enumerate((keep_ref, send_ref)):
        ref[...] = dg(mixed_ref[i * half : (i + 1) * half, :], w_ref[:, 0:hw], 1, 1).astype(BF)


def attn(s, sc, blocks, vec, shift, w):
    rows, width = blocks[0].shape[1:]
    seq, hw = 4 * rows, w.shape[1] // 4
    heads = hw // HD
    ins = (sc, *blocks, vec, shift, w)
    outs = [((seq, width), BF), ((seq, 4 * hw), BF), ((seq, hw), BF), ((8, seq), F32)]
    outs += [((2 * rows, width), BF)] * 2
    return call(
        functools.partial(attn_kernel, heads, rows, s), "attn_fwd", ins,
        [SM] + [VM] * 7, outs,
        [pltpu.VMEM((2, seq, seq), F32), pltpu.VMEM((2, seq, seq), BF)],
        2 * seq * width * 5 * hw + 16 * seq * seq * 128 * heads, heads * seq * seq,
    )


def attn_back_kernel(heads, rows, sc_ref, ga_ref, gb_ref, w_ref, qkv_ref, lse_ref,
                     gq_ref, keep_ref, send_ref, col_ref, s_ref, g_ref, p_ref, d_ref, gm_ref):
    seq = 4 * rows
    half = 2 * rows
    hw = heads * HD
    scale = HD**-0.5
    c = LOG2E * scale
    for i, ref in enumerate((ga_ref, gb_ref)):
        gm_ref[i * half : (i + 1) * half, :] = dg(ref[...], w_ref[:, 0:hw], 1, 0).astype(BF)
    lane = lax.broadcasted_iota(jnp.int32, (seq, 128), 1)
    pos = positions(sc_ref, rows, (seq, 128), 0)
    mask = jnp.where((lane == HD) & (pos >= sc_ref[1]), -1e30, 0.0).astype(BF)
    one = jnp.where(lane == HD, 1.0, 0.0).astype(BF)
    gq_ref[:, 0:hw] = jnp.zeros((seq, hw), BF)
    for h in range(heads):
        a = hw + HD * h
        qx = jnp.where(lane < HD, qkv_ref[:, a : a + 128], one)
        kx = jnp.where(lane < HD, qkv_ref[:, hw + a : hw + a + 128], mask)
        q = qkv_ref[:, a : a + HD]
        k = qkv_ref[:, hw + a : hw + a + HD]
        v = qkv_ref[:, 2 * hw + a : 2 * hw + a + HD]
        g = gm_ref[:, HD * h : HD * h + HD]
        sl = h % 2
        s_ref[sl] = dg(kx, qx, 1, 1)
        g_ref[sl] = dg(v, g, 1, 1)
        lse = lse_ref[h : h + 1, :]
        inner = jnp.zeros((CHUNK, seq), F32)
        for r in range(0, seq, CHUNK):
            p = jnp.exp2(s_ref[sl, r : r + CHUNK, :] * c - lse)
            s_ref[sl, r : r + CHUNK, :] = p
            p_ref[sl, r : r + CHUNK, :] = p.astype(BF)
            inner = inner + p * g_ref[sl, r : r + CHUNK, :]
        inner = jnp.sum(inner, 0, keepdims=True)
        for r in range(0, seq, CHUNK):
            d_ref[sl, r : r + CHUNK, :] = (
                s_ref[sl, r : r + CHUNK, :] * (g_ref[sl, r : r + CHUNK, :] - inner)
            ).astype(BF)
        gq_ref[:, a : a + HD] = (dg(k, d_ref[sl], 0, 0) * scale).T.astype(BF)
        gq_ref[:, hw + a : hw + a + HD] = (dg(d_ref[sl], q, 1, 0) * scale).astype(BF)
        gq_ref[:, 2 * hw + a : 2 * hw + a + HD] = dg(p_ref[sl], g, 1, 0).astype(BF)
    col = None
    for i, ref in enumerate((keep_ref, send_ref)):
        part = gq_ref[i * half : (i + 1) * half, :]
        ref[...] = dg(part, w_ref[...], 1, 1).astype(BF)
        now = jnp.sum(part.astype(F32), 0, keepdims=True)
        col = now if col is None else col + now
    col_ref[...] = col


def attn_back(sc, gml, w, qkv, lse):
    half, width = gml[0].shape
    seq, hw = 2 * half, w.shape[1] // 4
    heads = hw // HD
    ins = (sc, *gml, w, qkv, lse)
    outs = [((seq, 4 * hw), BF), ((half, width), BF), ((half, width), BF), ((1, 4 * hw), F32)]
    return call(
        functools.partial(attn_back_kernel, heads, half // 2), "attn_bwd", ins,
        [SM] + [VM] * 5, outs,
        [pltpu.VMEM((2, seq, seq), F32)] * 2 + [pltpu.VMEM((2, seq, seq), BF)] * 2
        + [pltpu.VMEM((seq, hw), BF)],
        2 * seq * width * 5 * hw + 24 * seq * seq * 128 * heads, heads * seq * seq,
    )


def mlp_kernel(rows, slot, sc_ref, na_ref, nb_ref, co, cf, cno, cnf, w_ref, ub_ref,
               act_ref, gh_ref, go_ref, okeep_ref, osend_ref, gkeep_ref, gsend_ref, us_ref):
    half = 2 * rows
    c0 = 0.7978845608028654
    limit = sc_ref[1]
    us = None
    units = ub_ref.shape[1]
    span = w_ref.shape[1] // 2
    wu_ref, wd_ref = w_ref.at[:, 0:units], w_ref.at[:, span : span + units]
    for i, (n_ref, pair, o_ref, g_ref) in enumerate((
        (na_ref, (co, cf), okeep_ref, gkeep_ref),
        (nb_ref, (cno, cnf), osend_ref, gsend_ref),
    )):
        parts = []
        for j, ref in enumerate(pair):
            start = (sc_ref[0] ^ ((0, 2, 1, 3)[2 * i + j])) * rows
            pos = lax.broadcasted_iota(jnp.int32, ref.shape[1:], 0) + start
            parts.append(jnp.where(pos < limit, ref[slot].astype(F32), 0.0))
        go = jnp.concatenate(parts, 0).astype(BF)
        go_ref[i * half : (i + 1) * half, :] = go
        hidden = dg(n_ref[...], wu_ref[...], 1, 0) + ub_ref[...]
        square = hidden * hidden
        t = jnp.tanh(hidden * (c0 + (c0 * 0.044715) * square))
        act = (0.5 * hidden * (1.0 + t)).astype(BF)
        slope = 0.5 * (1.0 + t) + hidden * (1.0 - t * t) * (0.5 * c0 + (1.5 * c0 * 0.044715) * square)
        act_ref[i * half : (i + 1) * half, :] = act
        o_ref[...] = dg(act, wd_ref[...], 1, 1).astype(BF)
        gh = (dg(go, wd_ref[...], 1, 0) * slope).astype(BF)
        gh_ref[i * half : (i + 1) * half, :] = gh
        g_ref[...] = dg(gh, wu_ref[...], 1, 1).astype(BF)
        now = jnp.sum(gh.astype(F32), 0, keepdims=True)
        us = now if us is None else us + now
    us_ref[...] = us


def mlp(s, sc, n2, blocks, w, ub):
    half, width = n2[0].shape
    rows, seq, units = half // 2, 2 * half, ub.shape[1]
    ins = (sc, *n2, *blocks, w, ub)
    outs = [((seq, units), BF), ((seq, units), BF), ((seq, width), BF)]
    outs += [((half, width), BF)] * 4 + [((1, units), F32)]
    return call(
        functools.partial(mlp_kernel, rows, s), "mlp", ins,
        [SM] + [VM] * 8, outs, [],
        8 * seq * width * units, seq * units,
    )


def pair_kernel(n, plan, pad, *refs):
    ins, out = refs[:n], refs[n]
    depth = out.shape[0]
    step = 384 if depth % 384 == 0 else depth
    for at, pairs in plan:
        for a in range(0, depth, step):
            total = None
            for l, r, first in pairs:
                right = ins[r][first : first + ins[l].shape[0], :]
                now = dg(ins[l][:, a : a + step], right, 0, 0)
                total = now if total is None else total + now
            if pad:
                fill = (-total.shape[1]) % 128
                total = jnp.concatenate([total, jnp.zeros((step, fill), F32)], 1)
            out[a : a + step, at : at + total.shape[1]] = total.astype(BF)


def weight_sums(name, depth, width, plan, pad=False, limit=56):
    ins, table, out, flops = [], {}, [], 0

    def index(x):
        if id(x) not in table:
            table[id(x)] = len(ins)
            ins.append(x)
        return table[id(x)]

    for at, pairs in plan:
        out.append((at, [(index(l), index(r), first) for l, r, first in pairs]))
        flops += sum(2 * l.shape[0] * l.shape[1] * r.shape[1] for l, r, _ in pairs)
    return call(
        functools.partial(pair_kernel, len(ins), out, pad), name, tuple(ins), [VM] * len(ins),
        [((depth, width), BF)], [], flops, limit=limit,
    )[0]


def middle_kernel(rows, slot, xo, xf, chip_ref, far_ref, vec_ref, mid_ref, n2_ref):
    parts = []
    for i, ref in enumerate((xo, xf)):
        a, b = i * rows, (1 - i) * rows
        mid = ref[slot].astype(F32) + (
            chip_ref[a : a + rows, :].astype(F32) + far_ref[b : b + rows, :].astype(F32)
        ) + vec_ref[2:3, :]
        mid_ref[a : a + rows, :] = mid
        parts.append(normal(mid)[0] * vec_ref[3:4, :] + vec_ref[4:5, :])
    n2_ref[...] = jnp.concatenate(parts, 0).astype(BF)


def middle_norm(s, xo, xf, chip, far, vec):
    half, width = chip.shape
    rows = half // 2
    return call(
        functools.partial(middle_kernel, rows, s), "middle_norm", (xo, xf, chip, far, vec),
        [VM] * 5, [((half, width), F32), ((half, width), BF)], [], 20 * half * width,
    )


def middle_back_kernel(rows, slot, sc_ref, co, cf, chip_ref, far_ref, mid_ref, vec_ref, gm_ref, gml_ref, sum_ref):
    parts = []
    for i, ref in enumerate((co, cf)):
        a, b = i * rows, (1 - i) * rows
        pos = lax.broadcasted_iota(jnp.int32, ref.shape[1:], 0) + (sc_ref[0] ^ (2 * i)) * rows
        go = jnp.where(pos < sc_ref[1], ref[slot].astype(F32), 0.0)
        grad = chip_ref[a : a + rows, :].astype(F32) + far_ref[b : b + rows, :].astype(F32)
        hat, inverse = normal(mid_ref[a : a + rows, :])
        gm = go + normal_back(hat, inverse, grad * vec_ref[3:4, :])
        parts.append(gm)
        if i == 0:
            gm_ref[...] = gm
            sum_ref[0:1, :] = jnp.sum(gm, 0, keepdims=True)
            sum_ref[1:2, :] = jnp.sum(hat * grad, 0, keepdims=True)
            sum_ref[2:3, :] = jnp.sum(grad, 0, keepdims=True)
            sum_ref[3:4, :] = jnp.sum(go, 0, keepdims=True)
    gml_ref[...] = jnp.concatenate(parts, 0).astype(BF)


def middle_back(s, sc, co, cf, chip, far, mid, vec):
    half, width = chip.shape
    rows = half // 2
    return call(
        functools.partial(middle_back_kernel, rows, s), "middle_bwd", (sc, co, cf, chip, far, mid, vec),
        [SM] + [VM] * 6,
        [((rows, width), F32), ((half, width), BF), ((4, width), F32)], [], 40 * half * width,
    )


def input_back_kernel(rows, slot, xo, keep_ref, near_ref, far_ref, gm_ref, vec_ref, out_ref, sum_ref):
    grad = (
        keep_ref[0:rows, :].astype(F32) + near_ref[0:rows, :].astype(F32) + far_ref[...].astype(F32)
    )
    hat, inverse = normal(xo[slot].astype(F32))
    out_ref[...] = gm_ref[...] + normal_back(hat, inverse, grad * vec_ref[0:1, :])
    sum_ref[0:1, :] = jnp.sum(hat * grad, 0, keepdims=True)
    sum_ref[1:2, :] = jnp.sum(grad, 0, keepdims=True)


def input_back(s, xo, keep, near, far, gm, vec):
    rows, width = far.shape
    return call(
        functools.partial(input_back_kernel, rows, s), "input_bwd", (xo, keep, near, far, gm, vec),
        [VM] * 6, [((rows, width), F32), ((2, width), F32)], [],
        30 * rows * width,
    )


def pack_attn_kernel(q_ref, k_ref, v_ref, o_ref, v0, v1, v2, v3, v4, v5, out_ref):
    shard, hw = q_ref.shape
    out_ref[0:shard, 0:hw] = o_ref[...].astype(F32).T.astype(BF)
    for i, ref in enumerate((q_ref, k_ref, v_ref)):
        out_ref[0:shard, (i + 1) * hw : (i + 2) * hw] = ref[...]
    lines = [ref[...].astype(F32) for ref in (v0, v1, v2, v3, v4, v5)]
    lines = jnp.concatenate(lines + [jnp.zeros((2, shard), F32)], 0)
    lines = jnp.concatenate([lines, jnp.zeros((8, 4 * hw - shard), F32)], 1)
    out_ref[shard : shard + 8, :] = lines.astype(BF)


def pack_mlp_kernel(u_ref, d_ref, out_ref):
    shard, units = u_ref.shape
    span = out_ref.shape[1] // 2
    fill = jnp.zeros((shard, span - units), F32)
    out_ref[:, 0:span] = jnp.concatenate([u_ref[...].astype(F32), fill], 1).astype(BF)
    out_ref[:, span:] = jnp.concatenate([d_ref[...].astype(F32).T, fill], 1).astype(BF)


def place_kernel(n, cuts, idx_ref, *refs):
    sources, outs, sems = refs[:n], refs[n:-1], refs[-1]
    copies = []
    for i, src in enumerate(sources):
        for o, (a, b) in enumerate(cuts):
            dst = outs[o].at[idx_ref[i]]
            copies.append(pltpu.make_async_copy(src.at[a:b], dst, sems.at[len(copies)]))
    for c in copies:
        c.start()
    for c in copies:
        c.wait()


def place_shards(idx, sources, cuts):
    n = len(sources)
    cols = sources[0].shape[1]
    outs = [((n, b - a, cols), BF) for a, b in cuts]
    return call(
        functools.partial(place_kernel, n, cuts), "place_shards", (idx, *sources), [SM] + [HBM] * n,
        outs, [pltpu.SemaphoreType.DMA((n * len(cuts),))], 0, limit=16,
    )


def after(x, *others):
    return lax.optimization_barrier((x, *others))[0]


def local(
    inputs,
    cotangent,
    lengths,
    ln1_gain,
    ln1_bias,
    q_weight,
    q_bias,
    k_weight,
    v_weight,
    v_bias,
    out_weight,
    out_bias,
    ln2_gain,
    ln2_bias,
    up_weight,
    up_bias,
    down_weight,
    down_bias,
):
    tp = lax.axis_size("tp")
    fs = lax.axis_size("fsdp")
    ti = lax.axis_index("tp")
    fi = lax.axis_index("fsdp")
    slots, rows, width = inputs.shape
    half = 2 * rows
    hw = q_weight.shape[1]
    units = up_weight.shape[1]
    shard = width // fs
    zi, yi = fi // 2, fi % 2

    def swap_tp(x, k):
        return lax.ppermute(x, "tp", [(i, i ^ k) for i in range(tp)])

    def swap_fs(x, k):
        return lax.ppermute(x, "fsdp", [(i, i ^ k) for i in range(fs)])

    def turn(x, k):
        return lax.ppermute(x, "fsdp", [(i, (i + 2 * k) % fs) for i in range(fs)])

    def gather_shards(own, cuts, beside, later):
        if fs != 8:
            whole = lax.all_gather(own, "fsdp", axis=0)
            return tuple(whole[:, a:b] for a, b in cuts), beside(own), later(own), whole
        first = lax.optimization_barrier((turn(own, 1), turn(own, 3), swap_fs(own, 1), beside(own)))
        r1, r3, o0, extra = first
        own, r1, r3, extra = lax.optimization_barrier((own, r1, r3, extra))
        second = (turn(own, 2), swap_fs(r1, 1), swap_fs(r3, 1), later(extra))
        r2, o1, o3, extra2 = lax.optimization_barrier(second)
        o2 = swap_fs(r2, 1)
        order = jnp.stack([(zi + 4 - k) % 4 for k in (0, 1, 3, 2)]) * 2
        idx = jnp.concatenate([order + yi, order + 1 - yi]).astype(jnp.int32)
        sources = [own, r1, r3, r2, o0, o1, o3, o2]
        return place_shards(idx, sources, cuts), extra, extra2, r1

    def scatter_sums(total):
        if fs != 8:
            return lax.psum_scatter(total, "fsdp", scatter_dimension=0, tiled=True).astype(F32)
        cols = total.shape[1]
        parts = total.reshape(4, 2, shard, cols)

        def pick(k, y):
            return lax.dynamic_slice(parts, ((zi + k) % 4, y, 0, 0), (1, 1, shard, cols))[0, 0]

        first = swap_fs(jnp.stack([pick(k, 1 - yi) for k in (1, 3, 2)], 0), 1)
        mine = swap_fs(pick(0, 1 - yi), 1)
        got = []
        for j, k in enumerate((1, 3, 2)):
            got.append(turn((pick(k, yi).astype(F32) + first[j].astype(F32)).astype(BF), k))
        mine = pick(0, yi).astype(F32) + mine.astype(F32)
        return mine + (got[0].astype(F32) + got[1].astype(F32)) + got[2].astype(F32)

    def chip_sum(keep, send):
        return (keep.astype(F32) + swap_tp(send, 1).astype(F32)).astype(BF)

    def own_part(keep, send):
        near = swap_tp(send, 1)
        far = (keep[rows:].astype(F32) + near[rows:].astype(F32)).astype(BF)
        return near, swap_tp(far, 2)

    lines = [a[None, :] for a in (ln1_gain, ln1_bias, out_bias, ln2_gain, ln2_bias, down_bias)]
    pack = call(
        pack_attn_kernel, "pack_attn", (q_weight, k_weight, v_weight, out_weight, *lines), [VM] * 10,
        [((shard + 8, 4 * hw), BF)], [], 0,
    )[0]
    (w_attn, small), x_far, c_far, sent = gather_shards(
        pack,
        ((0, shard), (shard, shard + 8)),
        lambda _: swap_tp(inputs, 2),
        lambda x: swap_tp(after(cotangent, x), 2),
    )
    x_blocks = (inputs, x_far, swap_tp(inputs, 1), swap_tp(x_far, 1))
    c_blocks = (cotangent, c_far, swap_tp(cotangent, 1), swap_tp(c_far, 1))
    w_attn = w_attn.reshape(width, 4 * hw)
    vec = small[:, :, :shard].transpose(1, 0, 2).reshape(8, width).astype(F32)
    span = units + (-units) % 128
    pack = call(
        pack_mlp_kernel, "pack_mlp", (up_weight, down_weight), [VM] * 2, [((shard, 2 * span), BF)], [], 0
    )[0]
    w_mlp = lax.all_gather(after(pack, sent), "fsdp", axis=0, tiled=True)

    none = jnp.zeros_like(q_bias)
    shift = jnp.concatenate([none, q_bias, none, v_bias], 0).astype(F32)[None, :]
    ub = up_bias.astype(F32)[None, :]
    scalars = [jnp.stack([ti, lengths[s]]).astype(jnp.int32) for s in range(slots)]

    every = range(slots)
    fwd, chips, mids, mlps = [], [], [], []
    w_now = w_attn
    for s in every:
        fwd.append(attn(s, scalars[s], x_blocks, vec, shift, w_now))
        chip = chip_sum(fwd[s][4], fwd[s][5])
        if s < slots - 1:
            chip, w_now = lax.optimization_barrier((chip, w_now))
        chips.append(chip)
    for s in every:
        mid, n2 = middle_norm(s, x_blocks[0], x_blocks[1], chips[s], swap_tp(chips[s], 2), vec)
        mids.append((mid, (n2, swap_tp(n2, 1))))
    chips = []
    w_now = w_mlp
    for s in every:
        mlps.append(mlp(s, scalars[s], mids[s][1], c_blocks, w_now, ub))
        chip = chip_sum(mlps[s][5], mlps[s][6])
        if s < slots - 1:
            chip, w_now = lax.optimization_barrier((chip, w_now))
        chips.append(chip)
    fars = [swap_tp(c, 2) for c in chips]
    ups, downs = [], []
    for s in every:
        act, gh, go = mlps[s][:3]
        if s == 0:
            act, fars[0] = lax.optimization_barrier((act, fars[0]))
        downs.append((go, act, 0))
        ups += [(mids[s][1][i], gh, i * half) for i in range(2)]
    g_mlp = weight_sums("mlp_dw", width, 2 * span, [(0, ups), (span, downs)], units % 128 > 0)
    r_mlp = lax.psum_scatter(g_mlp, "fsdp", scatter_dimension=0, tiled=True).astype(F32)
    outs, grads_x = [], []
    wide = cols = None
    heads_out, heads_in = [], []
    mid_now = [m[0] for m in mids]
    for s in every:
        okeep, osend = mlps[s][3:5]
        gm, gml, sums = middle_back(
            s, scalars[s], c_blocks[0], c_blocks[1], chips[s], fars[s], mid_now[s], vec
        )
        gml = (gml, swap_tp(gml, 1))
        n1, qkv, mixed, lse = fwd[s][:4]
        gqkv, keep, send, col = attn_back(scalars[s], gml, w_attn, qkv, lse)
        if s < slots - 1:
            mid_now[s + 1], col = lax.optimization_barrier((mid_now[s + 1], col))
        near, far = own_part(keep, send)
        grad, sums1 = input_back(s, x_blocks[0], keep, near, far, gm, vec)
        grads_x.append(grad)
        near, far = own_part(okeep, osend)
        outs.append(
            (
                mids[s][0][:rows]
                + (okeep[:rows].astype(F32) + near[:rows].astype(F32) + far.astype(F32))
                + vec[5:6]
            ).astype(BF)
        )
        now = jnp.concatenate([sums1, sums], 0)
        wide = now if wide is None else wide + now
        cols = col if cols is None else cols + col
        heads_out += [(gml[i], mixed, i * half) for i in range(2)]
        heads_in.append((n1, gqkv, 0))
    g_attn = weight_sums("attn_dw", width, 4 * hw, [(0, heads_in), (0, heads_out)])
    r_attn = scatter_sums(g_attn)

    unit_sums = sum(m[7] for m in mlps)
    wide = wide + swap_tp(wide, 1)
    wide = wide + swap_tp(wide, 2)
    flat = jnp.concatenate(
        [wide.reshape(-1), cols[0, hw : 2 * hw], cols[0, 3 * hw :], unit_sums[0]], 0
    )
    step = 1
    while step < fs:
        flat = flat + swap_fs(flat, step)
        step *= 2
    wide = flat[: 6 * width].reshape(6, width)
    wide = lax.dynamic_slice_in_dim(wide, fi * shard, shard, 1)
    tail = flat[6 * width :]
    return (
        jnp.stack(outs, 0),
        jnp.stack(grads_x, 0),
        wide[0],
        wide[1],
        r_attn[:, hw : 2 * hw],
        tail[:hw],
        r_attn[:, 2 * hw : 3 * hw],
        r_attn[:, 3 * hw :],
        tail[hw : 2 * hw],
        r_attn[:, :hw].T,
        wide[2],
        wide[3],
        wide[4],
        r_mlp[:, :units],
        tail[2 * hw :],
        r_mlp[:, span : span + units].T,
        wide[5],
    )


def solution(mesh):
    rowed = P("fsdp", "tp", None)
    wide = P("fsdp")
    cols = P("fsdp", "tp")
    turned = P("tp", "fsdp")
    part = P("tp")
    in_specs = (
        rowed, rowed, wide, wide, wide, cols, part, cols, cols, part, turned, wide,
        wide, wide, cols, part, turned, wide,
    )
    out_specs = (
        rowed, rowed, wide, wide, cols, part, cols, cols, part, turned, wide, wide, wide,
        cols, part, turned, wide,
    )
    return jax.shard_map(local, mesh=mesh, in_specs=in_specs, out_specs=out_specs, check_vma=False)
```

```python
import functools

import jax
import jax.numpy as jnp
from jax import lax
from jax.experimental import pallas as pl
from jax.experimental.pallas import tpu as pltpu
from jax.sharding import PartitionSpec as P

HD = 72
EPS = 1e-06
BF = jnp.bfloat16
F32 = jnp.float32
LOG2E = 1.4426950408889634
CHUNK = 16
VM = pl.BlockSpec(memory_space=pltpu.VMEM)
SM = pl.BlockSpec(memory_space=pltpu.SMEM)
HBM = pl.BlockSpec(memory_space=pl.ANY)


def dg(a, b, ca, cb):
    return lax.dot_general(a, b, (((ca,), (cb,)), ((), ())), preferred_element_type=F32)


def call(body, name, ins, specs, outs, scratch, flops, exps=0, limit=48):
    shapes = [jax.ShapeDtypeStruct(s, d) for s, d in outs]
    moved = sum(a.size * a.dtype.itemsize for a in ins)
    moved += sum(s.size * s.dtype.itemsize for s in shapes)
    return pl.pallas_call(
        body,
        out_shape=shapes,
        in_specs=specs,
        out_specs=[VM] * len(outs),
        scratch_shapes=scratch,
        compiler_params=pltpu.CompilerParams(vmem_limit_bytes=limit << 20),
        name=name,
        cost_estimate=pl.CostEstimate(
            flops=int(flops), bytes_accessed=int(moved), transcendentals=int(exps)
        ),
    )(*ins)


def staged(body, name, ins, modes, outs, out_modes, scratch, flops, exps=0, limit=44):
    shapes = [jax.ShapeDtypeStruct(s, d) for s, d in outs]
    kinds = {"S": SM, "V": VM}
    buffers, moves = [], 0
    for x, m in zip(ins, modes):
        if m not in ("S", "V", "A"):
            buffers.append(pltpu.VMEM(x.shape if m == "H" else x.shape[1:], x.dtype))
            moves += 1
    for (shape, kind), m in zip(outs, out_modes):
        if m == "H":
            buffers.append(pltpu.VMEM(shape, kind))
            moves += 4
    n_in, n_out, n_own = len(ins), len(outs), len(scratch)

    def kernel(*refs):
        in_refs, out_refs = refs[:n_in], refs[n_in : n_in + n_out]
        own = refs[n_in + n_out : n_in + n_out + n_own]
        spare = list(refs[n_in + n_out + n_own : -1])
        sems = refs[-1]
        used = []

        def copy(src, dst):
            c = pltpu.make_async_copy(src, dst, sems.at[len(used)])
            c.start()
            used.append(c)
            return c

        views, arriving, out_views, leaving = [], {}, [], []
        for i, (ref, m) in enumerate(zip(in_refs, modes)):
            if m in ("S", "V", "A"):
                views.append(ref)
            else:
                buf = spare.pop(0)
                arriving[i] = copy(ref if m == "H" else ref.at[m], buf)
                views.append(buf)
        for ref, m in zip(out_refs, out_modes):
            out_views.append(spare.pop(0) if m == "H" else ref)

        def ready(*which):
            for i in which:
                if i in arriving:
                    arriving.pop(i).wait()

        def leave(o, a, b):
            if out_modes[o] == "H":
                leaving.append(copy(out_views[o].at[a:b], out_refs[o].at[a:b]))

        body(ready, leave, *views, *out_views, *own)
        for c in leaving:
            c.wait()

    moved = sum(a.size * a.dtype.itemsize for a in ins) + sum(
        s.size * s.dtype.itemsize for s in shapes
    )
    return pl.pallas_call(
        kernel,
        out_shape=shapes,
        in_specs=[kinds.get(m, HBM) for m in modes],
        out_specs=[HBM if m == "H" else VM for m in out_modes],
        scratch_shapes=list(scratch) + buffers + [pltpu.SemaphoreType.DMA((max(moves, 1),))],
        compiler_params=pltpu.CompilerParams(vmem_limit_bytes=limit << 20),
        name=name,
        cost_estimate=pl.CostEstimate(
            flops=int(flops), bytes_accessed=int(moved), transcendentals=int(exps)
        ),
    )(*ins)


def normal(x):
    average = jnp.mean(x, -1, keepdims=True)
    center = x - average
    variance = jnp.mean(center * center, -1, keepdims=True)
    inverse = lax.rsqrt(variance + EPS)
    return center * inverse, inverse


def normal_back(hat, inverse, scaled):
    first = jnp.mean(scaled, -1, keepdims=True)
    second = jnp.mean(scaled * hat, -1, keepdims=True)
    return inverse * (scaled - first - hat * second)


def positions(sc_ref, rows, shape, dim):
    r = lax.broadcasted_iota(jnp.int32, shape, dim)
    ti = sc_ref[0]
    p0, p2, p1, p3 = ((ti ^ j) * rows for j in (0, 2, 1, 3))
    return jnp.where(
        r < 2 * rows,
        jnp.where(r < rows, r + p0, r + (p2 - rows)),
        jnp.where(r < 3 * rows, r + (p1 - 2 * rows), r + (p3 - 3 * rows)),
    )


def attn_kernel(heads, rows, slot, sc_ref, xo, xf, xno, xnf, vec_ref, shift_ref, w_ref,
                n1_ref, qkv_ref, mixed_ref, lse_ref, keep_ref, send_ref, s_ref, p_ref):
    seq = 4 * rows
    half = 2 * rows
    hw = heads * HD
    c = LOG2E * HD**-0.5
    gain, bias = vec_ref[0:1, :], vec_ref[1:2, :]
    for i, pair in enumerate(((xo, xf), (xno, xnf))):
        parts = [normal(ref[slot].astype(F32))[0] * gain + bias for ref in pair]
        n1 = jnp.concatenate(parts, 0).astype(BF)
        n1_ref[i * half : (i + 1) * half, :] = n1
        qkv_ref[i * half : (i + 1) * half, :] = (dg(n1, w_ref[...], 1, 0) + shift_ref[...]).astype(BF)
    lane = lax.broadcasted_iota(jnp.int32, (seq, 128), 1)
    pos = positions(sc_ref, rows, (seq, 128), 0)
    mask = jnp.where((lane == HD) & (pos >= sc_ref[1]), -1e30, 0.0).astype(BF)
    one = jnp.where(lane == HD, 1.0, 0.0).astype(BF)
    for h in range(heads):
        a = hw + HD * h
        qx = jnp.where(lane < HD, qkv_ref[:, a : a + 128], one)
        kx = jnp.where(lane < HD, qkv_ref[:, hw + a : hw + a + 128], mask)
        v = qkv_ref[:, 2 * hw + a : 2 * hw + a + HD]
        sl = h % 2
        s_ref[sl] = dg(kx, qx, 1, 1)
        m = s_ref[sl, 0:CHUNK, :]
        for r in range(CHUNK, seq, CHUNK):
            m = jnp.maximum(m, s_ref[sl, r : r + CHUNK, :])
        m = jnp.max(m, 0, keepdims=True) * c
        total = jnp.zeros((CHUNK, seq), F32)
        for r in range(0, seq, CHUNK):
            p = jnp.exp2(s_ref[sl, r : r + CHUNK, :] * c - m)
            total = total + p
            p_ref[sl, r : r + CHUNK, :] = p.astype(BF)
        total = jnp.sum(total, 0, keepdims=True)
        lse_ref[h : h + 1, :] = m + jnp.log2(total)
        mixed = dg(v, p_ref[sl], 0, 0) * (1.0 / total)
        mixed_ref[:, HD * h : HD * h + HD] = mixed.T.astype(BF)
    for i, ref in enumerate((keep_ref, send_ref)):
        ref[...] = dg(mixed_ref[i * half : (i + 1) * half, :], w_ref[:, 0:hw], 1, 1).astype(BF)


def attn(s, sc, blocks, vec, shift, w):
    rows, width = blocks[0].shape[1:]
    seq, hw = 4 * rows, w.shape[1] // 4
    heads = hw // HD
    ins = (sc, *blocks, vec, shift, w)
    outs = [((seq, width), BF), ((seq, 4 * hw), BF), ((seq, hw), BF), ((8, seq), F32)]
    outs += [((2 * rows, width), BF)] * 2
    return call(
        functools.partial(attn_kernel, heads, rows, s), "attn_fwd", ins,
        [SM] + [VM] * 7, outs,
        [pltpu.VMEM((2, seq, seq), F32), pltpu.VMEM((2, seq, seq), BF)],
        2 * seq * width * 5 * hw + 16 * seq * seq * 128 * heads, heads * seq * seq, limit=20,
    )


def attn_back_kernel(heads, rows, sc_ref, ga_ref, gb_ref, w_ref, qkv_ref, lse_ref,
                     gq_ref, keep_ref, send_ref, col_ref, s_ref, g_ref, p_ref, d_ref, gm_ref):
    seq = 4 * rows
    half = 2 * rows
    hw = heads * HD
    scale = HD**-0.5
    c = LOG2E * scale
    for i, ref in enumerate((ga_ref, gb_ref)):
        gm_ref[i * half : (i + 1) * half, :] = dg(ref[...], w_ref[:, 0:hw], 1, 0).astype(BF)
    lane = lax.broadcasted_iota(jnp.int32, (seq, 128), 1)
    pos = positions(sc_ref, rows, (seq, 128), 0)
    mask = jnp.where((lane == HD) & (pos >= sc_ref[1]), -1e30, 0.0).astype(BF)
    one = jnp.where(lane == HD, 1.0, 0.0).astype(BF)
    gq_ref[:, 0:hw] = jnp.zeros((seq, hw), BF)
    for h in range(heads):
        a = hw + HD * h
        qx = jnp.where(lane < HD, qkv_ref[:, a : a + 128], one)
        kx = jnp.where(lane < HD, qkv_ref[:, hw + a : hw + a + 128], mask)
        q = qkv_ref[:, a : a + HD]
        k = qkv_ref[:, hw + a : hw + a + HD]
        v = qkv_ref[:, 2 * hw + a : 2 * hw + a + HD]
        g = gm_ref[:, HD * h : HD * h + HD]
        sl = h % 2
        s_ref[sl] = dg(kx, qx, 1, 1)
        g_ref[sl] = dg(v, g, 1, 1)
        lse = lse_ref[h : h + 1, :]
        inner = jnp.zeros((CHUNK, seq), F32)
        for r in range(0, seq, CHUNK):
            p = jnp.exp2(s_ref[sl, r : r + CHUNK, :] * c - lse)
            s_ref[sl, r : r + CHUNK, :] = p
            p_ref[sl, r : r + CHUNK, :] = p.astype(BF)
            inner = inner + p * g_ref[sl, r : r + CHUNK, :]
        inner = jnp.sum(inner, 0, keepdims=True)
        for r in range(0, seq, CHUNK):
            d_ref[sl, r : r + CHUNK, :] = (
                s_ref[sl, r : r + CHUNK, :] * (g_ref[sl, r : r + CHUNK, :] - inner)
            ).astype(BF)
        gq_ref[:, a : a + HD] = (dg(k, d_ref[sl], 0, 0) * scale).T.astype(BF)
        gq_ref[:, hw + a : hw + a + HD] = (dg(d_ref[sl], q, 1, 0) * scale).astype(BF)
        gq_ref[:, 2 * hw + a : 2 * hw + a + HD] = dg(p_ref[sl], g, 1, 0).astype(BF)
    col = None
    for i, ref in enumerate((keep_ref, send_ref)):
        part = gq_ref[i * half : (i + 1) * half, :]
        ref[...] = dg(part, w_ref[...], 1, 1).astype(BF)
        now = jnp.sum(part.astype(F32), 0, keepdims=True)
        col = now if col is None else col + now
    col_ref[...] = col


def attn_back(sc, gml, w, qkv, lse):
    half, width = gml[0].shape
    seq, hw = 2 * half, w.shape[1] // 4
    heads = hw // HD
    ins = (sc, *gml, w, qkv, lse)
    outs = [((seq, 4 * hw), BF), ((half, width), BF), ((half, width), BF), ((1, 4 * hw), F32)]
    return call(
        functools.partial(attn_back_kernel, heads, half // 2), "attn_bwd", ins,
        [SM] + [VM] * 5, outs,
        [pltpu.VMEM((2, seq, seq), F32)] * 2 + [pltpu.VMEM((2, seq, seq), BF)] * 2
        + [pltpu.VMEM((seq, hw), BF)],
        2 * seq * width * 5 * hw + 24 * seq * seq * 128 * heads, heads * seq * seq, limit=30,
    )


def mlp_kernel(rows, slot, sc_ref, na_ref, nb_ref, co, cf, cno, cnf, w_ref, ub_ref,
               act_ref, gh_ref, go_ref, okeep_ref, osend_ref, gkeep_ref, gsend_ref, us_ref):
    half = 2 * rows
    c0 = 0.7978845608028654
    limit = sc_ref[1]
    us = None
    units = ub_ref.shape[1]
    span = w_ref.shape[1] // 2
    wu_ref, wd_ref = w_ref.at[:, 0:units], w_ref.at[:, span : span + units]
    for i, (n_ref, pair, o_ref, g_ref) in enumerate((
        (na_ref, (co, cf), okeep_ref, gkeep_ref),
        (nb_ref, (cno, cnf), osend_ref, gsend_ref),
    )):
        parts = []
        for j, ref in enumerate(pair):
            start = (sc_ref[0] ^ ((0, 2, 1, 3)[2 * i + j])) * rows
            pos = lax.broadcasted_iota(jnp.int32, ref.shape[1:], 0) + start
            parts.append(jnp.where(pos < limit, ref[slot].astype(F32), 0.0))
        go = jnp.concatenate(parts, 0).astype(BF)
        go_ref[i * half : (i + 1) * half, :] = go
        hidden = dg(n_ref[...], wu_ref[...], 1, 0) + ub_ref[...]
        square = hidden * hidden
        t = jnp.tanh(hidden * (c0 + (c0 * 0.044715) * square))
        act = (0.5 * hidden * (1.0 + t)).astype(BF)
        slope = 0.5 * (1.0 + t) + hidden * (1.0 - t * t) * (0.5 * c0 + (1.5 * c0 * 0.044715) * square)
        act_ref[i * half : (i + 1) * half, :] = act
        o_ref[...] = dg(act, wd_ref[...], 1, 1).astype(BF)
        gh = (dg(go, wd_ref[...], 1, 0) * slope).astype(BF)
        gh_ref[i * half : (i + 1) * half, :] = gh
        g_ref[...] = dg(gh, wu_ref[...], 1, 1).astype(BF)
        now = jnp.sum(gh.astype(F32), 0, keepdims=True)
        us = now if us is None else us + now
    us_ref[...] = us


def mlp(s, sc, n2, blocks, w, ub):
    half, width = n2[0].shape
    rows, seq, units = half // 2, 2 * half, ub.shape[1]
    ins = (sc, *n2, *blocks, w, ub)
    outs = [((seq, units), BF), ((seq, units), BF), ((seq, width), BF)]
    outs += [((half, width), BF)] * 4 + [((1, units), F32)]
    return call(
        functools.partial(mlp_kernel, rows, s), "mlp", ins,
        [SM] + [VM] * 8, outs, [],
        8 * seq * width * units, seq * units, limit=22,
    )


def pair_kernel(n, plan, pad, *refs):
    ins, out = refs[:n], refs[n]
    depth = out.shape[0]
    step = 384 if depth % 384 == 0 else depth
    for at, pairs in plan:
        for a in range(0, depth, step):
            total = None
            for l, r, first in pairs:
                right = ins[r][first : first + ins[l].shape[0], :]
                now = dg(ins[l][:, a : a + step], right, 0, 0)
                total = now if total is None else total + now
            if pad:
                fill = (-total.shape[1]) % 128
                total = jnp.concatenate([total, jnp.zeros((step, fill), F32)], 1)
            out[a : a + step, at : at + total.shape[1]] = total.astype(BF)


def weight_sums(name, depth, width, plan, pad=False, limit=23):
    ins, table, out, flops = [], {}, [], 0

    def index(x):
        if id(x) not in table:
            table[id(x)] = len(ins)
            ins.append(x)
        return table[id(x)]

    for at, pairs in plan:
        out.append((at, [(index(l), index(r), first) for l, r, first in pairs]))
        flops += sum(2 * l.shape[0] * l.shape[1] * r.shape[1] for l, r, _ in pairs)
    return call(
        functools.partial(pair_kernel, len(ins), out, pad), name, tuple(ins), [VM] * len(ins),
        [((depth, width), BF)], [], flops, limit=limit,
    )[0]


def middle_kernel(rows, slot, xo, xf, chip_ref, far_ref, vec_ref, mid_ref, n2_ref):
    parts = []
    for i, ref in enumerate((xo, xf)):
        a, b = i * rows, (1 - i) * rows
        mid = ref[slot].astype(F32) + (
            chip_ref[a : a + rows, :].astype(F32) + far_ref[b : b + rows, :].astype(F32)
        ) + vec_ref[2:3, :]
        mid_ref[a : a + rows, :] = mid
        parts.append(normal(mid)[0] * vec_ref[3:4, :] + vec_ref[4:5, :])
    n2_ref[...] = jnp.concatenate(parts, 0).astype(BF)


def middle_norm(s, xo, xf, chip, far, vec):
    half, width = chip.shape
    rows = half // 2
    return call(
        functools.partial(middle_kernel, rows, s), "middle_norm", (xo, xf, chip, far, vec),
        [VM] * 5, [((half, width), F32), ((half, width), BF)], [], 20 * half * width, limit=5,
    )


def middle_back_kernel(rows, slot, sc_ref, co, cf, chip_ref, far_ref, mid_ref, vec_ref, gm_ref, gml_ref, sum_ref):
    parts = []
    for i, ref in enumerate((co, cf)):
        a, b = i * rows, (1 - i) * rows
        pos = lax.broadcasted_iota(jnp.int32, ref.shape[1:], 0) + (sc_ref[0] ^ (2 * i)) * rows
        go = jnp.where(pos < sc_ref[1], ref[slot].astype(F32), 0.0)
        grad = chip_ref[a : a + rows, :].astype(F32) + far_ref[b : b + rows, :].astype(F32)
        hat, inverse = normal(mid_ref[a : a + rows, :])
        gm = go + normal_back(hat, inverse, grad * vec_ref[3:4, :])
        parts.append(gm)
        if i == 0:
            gm_ref[...] = gm
            sum_ref[0:1, :] = jnp.sum(gm, 0, keepdims=True)
            sum_ref[1:2, :] = jnp.sum(hat * grad, 0, keepdims=True)
            sum_ref[2:3, :] = jnp.sum(grad, 0, keepdims=True)
            sum_ref[3:4, :] = jnp.sum(go, 0, keepdims=True)
    gml_ref[...] = jnp.concatenate(parts, 0).astype(BF)


def middle_back(s, sc, co, cf, chip, far, mid, vec):
    half, width = chip.shape
    rows = half // 2
    return call(
        functools.partial(middle_back_kernel, rows, s), "middle_bwd", (sc, co, cf, chip, far, mid, vec),
        [SM] + [VM] * 6,
        [((rows, width), F32), ((half, width), BF), ((4, width), F32)], [], 40 * half * width, limit=10,
    )


def input_back_kernel(rows, slot, xo, keep_ref, near_ref, far_ref, gm_ref, vec_ref, out_ref, sum_ref):
    grad = (
        keep_ref[0:rows, :].astype(F32) + near_ref[0:rows, :].astype(F32) + far_ref[...].astype(F32)
    )
    hat, inverse = normal(xo[slot].astype(F32))
    out_ref[...] = gm_ref[...] + normal_back(hat, inverse, grad * vec_ref[0:1, :])
    sum_ref[0:1, :] = jnp.sum(hat * grad, 0, keepdims=True)
    sum_ref[1:2, :] = jnp.sum(grad, 0, keepdims=True)


def input_back(s, xo, keep, near, far, gm, vec):
    rows, width = far.shape
    return call(
        functools.partial(input_back_kernel, rows, s), "input_bwd", (xo, keep, near, far, gm, vec),
        [VM] * 6, [((rows, width), F32), ((2, width), F32)], [],
        30 * rows * width, limit=5,
    )


def pack_attn_kernel(*refs):
    ins, out_ref, held, lines, sems = refs[:10], refs[10], refs[11:15], refs[15:21], refs[21]
    copies = [
        pltpu.make_async_copy(src, dst, sems.at[i]) for i, (src, dst) in enumerate(zip(ins, held + lines))
    ]
    for copy in copies:
        copy.start()
    for copy in copies:
        copy.wait()
    shard, hw = held[0].shape
    out_ref[0:shard, 0:hw] = held[3][...].astype(F32).T.astype(BF)
    for i in range(3):
        out_ref[0:shard, (i + 1) * hw : (i + 2) * hw] = held[i][...]
    rows = [ref[...].astype(F32).reshape(1, shard) for ref in lines]
    rows = jnp.concatenate(rows + [jnp.zeros((2, shard), F32)], 0)
    rows = jnp.concatenate([rows, jnp.zeros((8, 4 * hw - shard), F32)], 1)
    out_ref[shard : shard + 8, :] = rows.astype(BF)


def pack_mlp_kernel(ready, leave, u_ref, d_ref, out_ref):
    ready(0, 1)
    shard, units = u_ref.shape
    span = out_ref.shape[1] // 2
    fill = jnp.zeros((shard, span - units), F32)
    out_ref[:, 0:span] = jnp.concatenate([u_ref[...].astype(F32), fill], 1).astype(BF)
    out_ref[:, span:] = jnp.concatenate([d_ref[...].astype(F32).T, fill], 1).astype(BF)


def place_kernel(n, cuts, idx_ref, *refs):
    sources, outs, sems = refs[:n], refs[n:-1], refs[-1]
    copies = []
    for i, src in enumerate(sources):
        for o, (a, b) in enumerate(cuts):
            dst = outs[o].at[idx_ref[i]]
            copies.append(pltpu.make_async_copy(src.at[a:b], dst, sems.at[len(copies)]))
    for c in copies:
        c.start()
    for c in copies:
        c.wait()


def place_shards(idx, sources, cuts):
    n = len(sources)
    cols = sources[0].shape[1]
    outs = [((n, b - a, cols), BF) for a, b in cuts]
    return call(
        functools.partial(place_kernel, n, cuts), "place_shards", (idx, *sources), [SM] + [HBM] * n,
        outs, [pltpu.SemaphoreType.DMA((n * len(cuts),))], 0, limit=6,
    )


def close_kernel(n, *refs):
    total = refs[0][...].astype(F32)
    for ref in refs[1:n]:
        total = total + ref[...].astype(F32)
    hw = total.shape[1] // 4
    for i in range(3):
        refs[n + i][...] = total[:, (i + 1) * hw : (i + 2) * hw]
    refs[n + 3][...] = total[:, 0:hw].T


def close_sums(parts, hw):
    rows, n = parts[0].shape[0], len(parts)
    return call(
        functools.partial(close_kernel, n), "close_sums", tuple(parts), [VM] * n,
        [((rows, hw), F32)] * 3 + [((hw, rows), F32)], [], 8 * rows * hw * n, limit=8,
    )


def after(x, *others):
    return lax.optimization_barrier((x, *others))[0]


def local(
    inputs,
    cotangent,
    lengths,
    ln1_gain,
    ln1_bias,
    q_weight,
    q_bias,
    k_weight,
    v_weight,
    v_bias,
    out_weight,
    out_bias,
    ln2_gain,
    ln2_bias,
    up_weight,
    up_bias,
    down_weight,
    down_bias,
):
    tp = lax.axis_size("tp")
    fs = lax.axis_size("fsdp")
    ti = lax.axis_index("tp")
    fi = lax.axis_index("fsdp")
    slots, rows, width = inputs.shape
    half = 2 * rows
    hw = q_weight.shape[1]
    units = up_weight.shape[1]
    shard = width // fs
    zi, yi = fi // 2, fi % 2

    def swap_tp(x, k):
        return lax.ppermute(x, "tp", [(i, i ^ k) for i in range(tp)])

    def swap_fs(x, k):
        return lax.ppermute(x, "fsdp", [(i, i ^ k) for i in range(fs)])

    def turn(x, k):
        return lax.ppermute(x, "fsdp", [(i, (i + 2 * k) % fs) for i in range(fs)])

    def gather_shards(own, cuts, beside, later):
        if fs != 8:
            whole = lax.all_gather(own, "fsdp", axis=0)
            return tuple(whole[:, a:b] for a, b in cuts), beside(own), later(own), whole
        first = lax.optimization_barrier((turn(own, 1), turn(own, 3), swap_fs(own, 1), beside(own)))
        r1, r3, o0, extra = first
        own, r1, r3, extra = lax.optimization_barrier((own, r1, r3, extra))
        second = (turn(own, 2), swap_fs(r1, 1), swap_fs(r3, 1), later(extra))
        r2, o1, o3, extra2 = lax.optimization_barrier(second)
        o2 = swap_fs(r2, 1)
        order = jnp.stack([(zi + 4 - k) % 4 for k in (0, 1, 3, 2)]) * 2
        idx = jnp.concatenate([order + yi, order + 1 - yi]).astype(jnp.int32)
        sources = [own, r1, r3, r2, o0, o1, o3, o2]
        return place_shards(idx, sources, cuts), extra, extra2, r1

    def scatter_sums(total, beside):
        if fs != 8:
            return [lax.psum_scatter(total, "fsdp", scatter_dimension=0, tiled=True)], beside
        cols = total.shape[1]
        parts = total.reshape(4, 2, shard, cols)

        def pick(k, y):
            return lax.dynamic_slice(parts, ((zi + k) % 4, y, 0, 0), (1, 1, shard, cols))[0, 0]

        first = swap_fs(jnp.stack([pick(k, 1 - yi) for k in (1, 3, 2)], 0), 1)
        mine = swap_fs(pick(0, 1 - yi), 1)
        sums = [(pick(k, yi).astype(F32) + first[j].astype(F32)).astype(BF) for j, k in enumerate((1, 3, 2))]
        *sums, beside = lax.optimization_barrier((*sums, beside))
        got = [turn(a, k) for a, k in zip(sums, (1, 3, 2))]
        return [pick(0, yi), mine, *got], beside

    def chip_sum(keep, send):
        return (keep.astype(F32) + swap_tp(send, 1).astype(F32)).astype(BF)

    def own_part(keep, send):
        near = swap_tp(send, 1)
        far = (keep[rows:].astype(F32) + near[rows:].astype(F32)).astype(BF)
        return near, swap_tp(far, 2)

    shards = (q_weight, k_weight, v_weight, out_weight)
    lines = (ln1_gain, ln1_bias, out_bias, ln2_gain, ln2_bias, down_bias)
    pack = call(
        pack_attn_kernel, "pack_attn", (*shards, *lines), [HBM] * 10, [((shard + 8, 4 * hw), BF)],
        [pltpu.VMEM(a.shape, BF) for a in shards + lines] + [pltpu.SemaphoreType.DMA((10,))], 0, limit=60,
    )[0]
    (w_attn, small), x_far, c_far, sent = gather_shards(
        pack,
        ((0, shard), (shard, shard + 8)),
        lambda _: swap_tp(inputs, 2),
        lambda x: swap_tp(after(cotangent, x), 2),
    )
    x_blocks = (inputs, x_far, swap_tp(inputs, 1), swap_tp(x_far, 1))
    c_blocks = (cotangent, c_far, swap_tp(cotangent, 1), swap_tp(c_far, 1))
    w_attn = w_attn.reshape(width, 4 * hw)
    vec = small[:, :, :shard].transpose(1, 0, 2).reshape(8, width).astype(F32)
    span = units + (-units) % 128
    pack = staged(
        pack_mlp_kernel, "pack_mlp", (up_weight, down_weight), ["H", "H"], [((shard, 2 * span), BF)],
        ["V"], [], 0, limit=60
    )[0]
    w_mlp = lax.all_gather(after(pack, sent), "fsdp", axis=0, tiled=True)

    none = jnp.zeros_like(q_bias)
    shift = jnp.concatenate([none, q_bias, none, v_bias], 0).astype(F32)[None, :]
    ub = up_bias.astype(F32)[None, :]
    scalars = [jnp.stack([ti, lengths[s]]).astype(jnp.int32) for s in range(slots)]

    every = range(slots)
    fwd, chips, mids, mlps = [], [], [], []
    w_now = w_attn
    for s in every:
        fwd.append(attn(s, scalars[s], x_blocks, vec, shift, w_now))
        chip = chip_sum(fwd[s][4], fwd[s][5])
        if s < slots - 1:
            chip, w_now = lax.optimization_barrier((chip, w_now))
        chips.append(chip)
    for s in every:
        mid, n2 = middle_norm(s, x_blocks[0], x_blocks[1], chips[s], swap_tp(chips[s], 2), vec)
        mids.append((mid, (n2, swap_tp(n2, 1))))
    chips = []
    w_now = w_mlp
    for s in every:
        mlps.append(mlp(s, scalars[s], mids[s][1], c_blocks, w_now, ub))
        chip = chip_sum(mlps[s][5], mlps[s][6])
        if s < slots - 1:
            chip, w_now = lax.optimization_barrier((chip, w_now))
        chips.append(chip)
    fars = [swap_tp(c, 2) for c in chips]
    ups, downs = [], []
    for s in every:
        act, gh, go = mlps[s][:3]
        if s == 0:
            act, fars[0] = lax.optimization_barrier((act, fars[0]))
        downs.append((go, act, 0))
        ups += [(mids[s][1][i], gh, i * half) for i in range(2)]
    g_mlp = weight_sums("mlp_dw", width, 2 * span, [(0, ups), (span, downs)], units % 128 > 0)
    r_mlp = lax.psum_scatter(g_mlp, "fsdp", scatter_dimension=0, tiled=True).astype(F32)
    outs, grads_x = [], []
    wide = cols = None
    heads_out, heads_in = [], []
    mid_now = [m[0] for m in mids]
    for s in every:
        okeep, osend = mlps[s][3:5]
        gm, gml, sums = middle_back(
            s, scalars[s], c_blocks[0], c_blocks[1], chips[s], fars[s], mid_now[s], vec
        )
        gml = (gml, swap_tp(gml, 1))
        n1, qkv, mixed, lse = fwd[s][:4]
        gqkv, keep, send, col = attn_back(scalars[s], gml, w_attn, qkv, lse)
        if s < slots - 1:
            mid_now[s + 1], col = lax.optimization_barrier((mid_now[s + 1], col))
        near, far = own_part(keep, send)
        grad, sums1 = input_back(s, x_blocks[0], keep, near, far, gm, vec)
        grads_x.append(grad)
        near, far = own_part(okeep, osend)
        outs.append(
            (
                mids[s][0][:rows]
                + (okeep[:rows].astype(F32) + near[:rows].astype(F32) + far.astype(F32))
                + vec[5:6]
            ).astype(BF)
        )
        now = jnp.concatenate([sums1, sums], 0)
        wide = now if wide is None else wide + now
        cols = col if cols is None else cols + col
        heads_out += [(gml[i], mixed, i * half) for i in range(2)]
        heads_in.append((n1, gqkv, 0))
    g_attn = weight_sums("attn_dw", width, 4 * hw, [(0, heads_in), (0, heads_out)])

    unit_sums = sum(m[7] for m in mlps)
    wide = wide + swap_tp(wide, 1)
    wide = wide + swap_tp(wide, 2)
    flat = jnp.concatenate(
        [wide.reshape(-1), cols[0, hw : 2 * hw], cols[0, 3 * hw :], unit_sums[0]], 0
    )
    step = 1
    while step < fs:
        flat = flat + swap_fs(flat, step)
        step *= 2
    parts, flat = scatter_sums(g_attn, flat)
    gq, gk, gv, go = close_sums(parts, hw)
    wide = flat[: 6 * width].reshape(6, width)
    wide = lax.dynamic_slice_in_dim(wide, fi * shard, shard, 1)
    tail = flat[6 * width :]
    return (
        jnp.stack(outs, 0),
        jnp.stack(grads_x, 0),
        wide[0],
        wide[1],
        gq,
        tail[:hw],
        gk,
        gv,
        tail[hw : 2 * hw],
        go,
        wide[2],
        wide[3],
        wide[4],
        r_mlp[:, :units],
        tail[2 * hw :],
        r_mlp[:, span : span + units].T,
        wide[5],
    )


def solution(mesh):
    rowed = P("fsdp", "tp", None)
    wide = P("fsdp")
    cols = P("fsdp", "tp")
    turned = P("tp", "fsdp")
    part = P("tp")
    in_specs = (
        rowed, rowed, wide, wide, wide, cols, part, cols, cols, part, turned, wide,
        wide, wide, cols, part, turned, wide,
    )
    out_specs = (
        rowed, rowed, wide, wide, cols, part, cols, cols, part, turned, wide, wide, wide,
        cols, part, turned, wide,
    )
    return jax.shard_map(local, mesh=mesh, in_specs=in_specs, out_specs=out_specs, check_vma=False)
```

```python
import functools

import jax
import jax.numpy as jnp
from jax import lax
from jax.experimental import pallas as pl
from jax.experimental.pallas import tpu as pltpu
from jax.sharding import PartitionSpec as P

HD = 72
EPS = 1e-06
BF = jnp.bfloat16
F32 = jnp.float32
LOG2E = 1.4426950408889634
CHUNK = 16
VM = pl.BlockSpec(memory_space=pltpu.VMEM)
SM = pl.BlockSpec(memory_space=pltpu.SMEM)
HBM = pl.BlockSpec(memory_space=pl.ANY)


def dg(a, b, ca, cb):
    return lax.dot_general(a, b, (((ca,), (cb,)), ((), ())), preferred_element_type=F32)


def call(body, name, ins, specs, outs, scratch, flops, exps=0, limit=48):
    shapes = [jax.ShapeDtypeStruct(s, d) for s, d in outs]
    moved = sum(a.size * a.dtype.itemsize for a in ins)
    moved += sum(s.size * s.dtype.itemsize for s in shapes)
    return pl.pallas_call(
        body,
        out_shape=shapes,
        in_specs=specs,
        out_specs=[VM] * len(outs),
        scratch_shapes=scratch,
        compiler_params=pltpu.CompilerParams(vmem_limit_bytes=limit << 20),
        name=name,
        cost_estimate=pl.CostEstimate(
            flops=int(flops), bytes_accessed=int(moved), transcendentals=int(exps)
        ),
    )(*ins)


def staged(body, name, ins, modes, outs, out_modes, scratch, flops, exps=0, limit=44):
    shapes = [jax.ShapeDtypeStruct(s, d) for s, d in outs]
    kinds = {"S": SM, "V": VM}
    buffers, moves = [], 0
    for x, m in zip(ins, modes):
        if m not in ("S", "V", "A"):
            buffers.append(pltpu.VMEM(x.shape if m == "H" else x.shape[1:], x.dtype))
            moves += 1
    for (shape, kind), m in zip(outs, out_modes):
        if m == "H":
            buffers.append(pltpu.VMEM(shape, kind))
            moves += 4
    n_in, n_out, n_own = len(ins), len(outs), len(scratch)

    def kernel(*refs):
        in_refs, out_refs = refs[:n_in], refs[n_in : n_in + n_out]
        own = refs[n_in + n_out : n_in + n_out + n_own]
        spare = list(refs[n_in + n_out + n_own : -1])
        sems = refs[-1]
        used = []

        def copy(src, dst):
            c = pltpu.make_async_copy(src, dst, sems.at[len(used)])
            c.start()
            used.append(c)
            return c

        views, arriving, out_views, leaving = [], {}, [], []
        for i, (ref, m) in enumerate(zip(in_refs, modes)):
            if m in ("S", "V", "A"):
                views.append(ref)
            else:
                buf = spare.pop(0)
                arriving[i] = copy(ref if m == "H" else ref.at[m], buf)
                views.append(buf)
        for ref, m in zip(out_refs, out_modes):
            out_views.append(spare.pop(0) if m == "H" else ref)

        def ready(*which):
            for i in which:
                if i in arriving:
                    arriving.pop(i).wait()

        def leave(o, a, b):
            if out_modes[o] == "H":
                leaving.append(copy(out_views[o].at[a:b], out_refs[o].at[a:b]))

        body(ready, leave, *views, *out_views, *own)
        for c in leaving:
            c.wait()

    moved = sum(a.size * a.dtype.itemsize for a in ins) + sum(
        s.size * s.dtype.itemsize for s in shapes
    )
    return pl.pallas_call(
        kernel,
        out_shape=shapes,
        in_specs=[kinds.get(m, HBM) for m in modes],
        out_specs=[HBM if m == "H" else VM for m in out_modes],
        scratch_shapes=list(scratch) + buffers + [pltpu.SemaphoreType.DMA((max(moves, 1),))],
        compiler_params=pltpu.CompilerParams(vmem_limit_bytes=limit << 20),
        name=name,
        cost_estimate=pl.CostEstimate(
            flops=int(flops), bytes_accessed=int(moved), transcendentals=int(exps)
        ),
    )(*ins)


def normal(x):
    average = jnp.mean(x, -1, keepdims=True)
    center = x - average
    variance = jnp.mean(center * center, -1, keepdims=True)
    inverse = lax.rsqrt(variance + EPS)
    return center * inverse, inverse


def normal_back(hat, inverse, scaled):
    first = jnp.mean(scaled, -1, keepdims=True)
    second = jnp.mean(scaled * hat, -1, keepdims=True)
    return inverse * (scaled - first - hat * second)


def positions(sc_ref, rows, shape, dim):
    r = lax.broadcasted_iota(jnp.int32, shape, dim)
    ti = sc_ref[0]
    p0, p2, p1, p3 = ((ti ^ j) * rows for j in (0, 2, 1, 3))
    return jnp.where(
        r < 2 * rows,
        jnp.where(r < rows, r + p0, r + (p2 - rows)),
        jnp.where(r < 3 * rows, r + (p1 - 2 * rows), r + (p3 - 3 * rows)),
    )


def attn_kernel(heads, rows, slot, sc_ref, xo, xf, xno, xnf, vec_ref, shift_ref, w_ref,
                n1_ref, qkv_ref, mixed_ref, lse_ref, keep_ref, send_ref, s_ref, p_ref):
    seq = 4 * rows
    half = 2 * rows
    hw = heads * HD
    c = LOG2E * HD**-0.5
    gain, bias = vec_ref[0:1, :], vec_ref[1:2, :]
    for i, pair in enumerate(((xo, xf), (xno, xnf))):
        parts = [normal(ref[slot].astype(F32))[0] * gain + bias for ref in pair]
        n1 = jnp.concatenate(parts, 0).astype(BF)
        n1_ref[i * half : (i + 1) * half, :] = n1
        qkv_ref[i * half : (i + 1) * half, :] = (dg(n1, w_ref[...], 1, 0) + shift_ref[...]).astype(BF)
    lane = lax.broadcasted_iota(jnp.int32, (seq, 128), 1)
    pos = positions(sc_ref, rows, (seq, 128), 0)
    mask = jnp.where((lane == HD) & (pos >= sc_ref[1]), -1e30, 0.0).astype(BF)
    one = jnp.where(lane == HD, 1.0, 0.0).astype(BF)
    for h in range(heads):
        a = hw + HD * h
        qx = jnp.where(lane < HD, qkv_ref[:, a : a + 128], one)
        kx = jnp.where(lane < HD, qkv_ref[:, hw + a : hw + a + 128], mask)
        v = qkv_ref[:, 2 * hw + a : 2 * hw + a + HD]
        sl = h % 2
        s_ref[sl] = dg(kx, qx, 1, 1)
        m = s_ref[sl, 0:CHUNK, :]
        for r in range(CHUNK, seq, CHUNK):
            m = jnp.maximum(m, s_ref[sl, r : r + CHUNK, :])
        m = jnp.max(m, 0, keepdims=True) * c
        total = jnp.zeros((CHUNK, seq), F32)
        for r in range(0, seq, CHUNK):
            p = jnp.exp2(s_ref[sl, r : r + CHUNK, :] * c - m)
            total = total + p
            p_ref[sl, r : r + CHUNK, :] = p.astype(BF)
        total = jnp.sum(total, 0, keepdims=True)
        lse_ref[h : h + 1, :] = m + jnp.log2(total)
        mixed = dg(v, p_ref[sl], 0, 0) * (1.0 / total)
        mixed_ref[:, HD * h : HD * h + HD] = mixed.T.astype(BF)
    for i, ref in enumerate((keep_ref, send_ref)):
        ref[...] = dg(mixed_ref[i * half : (i + 1) * half, :], w_ref[:, 0:hw], 1, 1).astype(BF)


def attn(s, sc, blocks, vec, shift, w):
    rows, width = blocks[0].shape[1:]
    seq, hw = 4 * rows, w.shape[1] // 4
    heads = hw // HD
    ins = (sc, *blocks, vec, shift, w)
    outs = [((seq, width), BF), ((seq, 4 * hw), BF), ((seq, hw), BF), ((8, seq), F32)]
    outs += [((2 * rows, width), BF)] * 2
    return call(
        functools.partial(attn_kernel, heads, rows, s), "attn_fwd", ins,
        [SM] + [VM] * 7, outs,
        [pltpu.VMEM((2, seq, seq), F32), pltpu.VMEM((2, seq, seq), BF)],
        2 * seq * width * 5 * hw + 16 * seq * seq * 128 * heads, heads * seq * seq, limit=20,
    )


def attn_back_kernel(heads, rows, sc_ref, ga_ref, gb_ref, w_ref, qkv_ref, lse_ref,
                     gq_ref, keep_ref, send_ref, col_ref, s_ref, g_ref, p_ref, d_ref, gm_ref):
    seq = 4 * rows
    half = 2 * rows
    hw = heads * HD
    scale = HD**-0.5
    c = LOG2E * scale
    for i, ref in enumerate((ga_ref, gb_ref)):
        gm_ref[i * half : (i + 1) * half, :] = dg(ref[...], w_ref[:, 0:hw], 1, 0).astype(BF)
    lane = lax.broadcasted_iota(jnp.int32, (seq, 128), 1)
    pos = positions(sc_ref, rows, (seq, 128), 0)
    mask = jnp.where((lane == HD) & (pos >= sc_ref[1]), -1e30, 0.0).astype(BF)
    one = jnp.where(lane == HD, 1.0, 0.0).astype(BF)
    gq_ref[:, 0:hw] = jnp.zeros((seq, hw), BF)
    for h in range(heads):
        a = hw + HD * h
        qx = jnp.where(lane < HD, qkv_ref[:, a : a + 128], one)
        kx = jnp.where(lane < HD, qkv_ref[:, hw + a : hw + a + 128], mask)
        q = qkv_ref[:, a : a + HD]
        k = qkv_ref[:, hw + a : hw + a + HD]
        v = qkv_ref[:, 2 * hw + a : 2 * hw + a + HD]
        g = gm_ref[:, HD * h : HD * h + HD]
        sl = h % 2
        s_ref[sl] = dg(kx, qx, 1, 1)
        g_ref[sl] = dg(v, g, 1, 1)
        lse = lse_ref[h : h + 1, :]
        inner = jnp.zeros((CHUNK, seq), F32)
        for r in range(0, seq, CHUNK):
            p = jnp.exp2(s_ref[sl, r : r + CHUNK, :] * c - lse)
            s_ref[sl, r : r + CHUNK, :] = p
            p_ref[sl, r : r + CHUNK, :] = p.astype(BF)
            inner = inner + p * g_ref[sl, r : r + CHUNK, :]
        inner = jnp.sum(inner, 0, keepdims=True)
        for r in range(0, seq, CHUNK):
            d_ref[sl, r : r + CHUNK, :] = (
                s_ref[sl, r : r + CHUNK, :] * (g_ref[sl, r : r + CHUNK, :] - inner)
            ).astype(BF)
        gq_ref[:, a : a + HD] = (dg(k, d_ref[sl], 0, 0) * scale).T.astype(BF)
        gq_ref[:, hw + a : hw + a + HD] = (dg(d_ref[sl], q, 1, 0) * scale).astype(BF)
        gq_ref[:, 2 * hw + a : 2 * hw + a + HD] = dg(p_ref[sl], g, 1, 0).astype(BF)
    col = None
    for i, ref in enumerate((keep_ref, send_ref)):
        part = gq_ref[i * half : (i + 1) * half, :]
        ref[...] = dg(part, w_ref[...], 1, 1).astype(BF)
        now = jnp.sum(part.astype(F32), 0, keepdims=True)
        col = now if col is None else col + now
    col_ref[...] = col


def attn_back(sc, gml, w, qkv, lse):
    half, width = gml[0].shape
    seq, hw = 2 * half, w.shape[1] // 4
    heads = hw // HD
    ins = (sc, *gml, w, qkv, lse)
    outs = [((seq, 4 * hw), BF), ((half, width), BF), ((half, width), BF), ((1, 4 * hw), F32)]
    return call(
        functools.partial(attn_back_kernel, heads, half // 2), "attn_bwd", ins,
        [SM] + [VM] * 5, outs,
        [pltpu.VMEM((2, seq, seq), F32)] * 2 + [pltpu.VMEM((2, seq, seq), BF)] * 2
        + [pltpu.VMEM((seq, hw), BF)],
        2 * seq * width * 5 * hw + 24 * seq * seq * 128 * heads, heads * seq * seq, limit=30,
    )


def mlp_kernel(rows, slot, sc_ref, na_ref, nb_ref, co, cf, cno, cnf, w_ref, ub_ref,
               act_ref, gh_ref, go_ref, okeep_ref, osend_ref, gkeep_ref, gsend_ref, us_ref):
    half = 2 * rows
    c0 = 0.7978845608028654
    limit = sc_ref[1]
    us = None
    units = ub_ref.shape[1]
    main = units - units % 128
    wu_ref = w_ref.at[:, 0:units]
    wa_ref, wb_ref = w_ref.at[:, main + 128 :], w_ref.at[:, units : 2 * units - main]
    for i, (n_ref, pair, o_ref, g_ref) in enumerate((
        (na_ref, (co, cf), okeep_ref, gkeep_ref),
        (nb_ref, (cno, cnf), osend_ref, gsend_ref),
    )):
        parts = []
        for j, ref in enumerate(pair):
            start = (sc_ref[0] ^ ((0, 2, 1, 3)[2 * i + j])) * rows
            pos = lax.broadcasted_iota(jnp.int32, ref.shape[1:], 0) + start
            parts.append(jnp.where(pos < limit, ref[slot].astype(F32), 0.0))
        go = jnp.concatenate(parts, 0).astype(BF)
        go_ref[i * half : (i + 1) * half, :] = go
        hidden = dg(n_ref[...], wu_ref[...], 1, 0) + ub_ref[...]
        square = hidden * hidden
        t = jnp.tanh(hidden * (c0 + (c0 * 0.044715) * square))
        act = (0.5 * hidden * (1.0 + t)).astype(BF)
        slope = 0.5 * (1.0 + t) + hidden * (1.0 - t * t) * (0.5 * c0 + (1.5 * c0 * 0.044715) * square)
        act_ref[i * half : (i + 1) * half, :] = act
        o_ref[...] = (
            dg(act[:, 0:main], wa_ref[...], 1, 1) + dg(act[:, main:], wb_ref[...], 1, 1)
        ).astype(BF)
        grad = jnp.concatenate([dg(go, wa_ref[...], 1, 0), dg(go, wb_ref[...], 1, 0)], 1)
        gh = (grad * slope).astype(BF)
        gh_ref[i * half : (i + 1) * half, :] = gh
        g_ref[...] = dg(gh, wu_ref[...], 1, 1).astype(BF)
        now = jnp.sum(gh.astype(F32), 0, keepdims=True)
        us = now if us is None else us + now
    us_ref[...] = us


def mlp(s, sc, n2, blocks, w, ub):
    half, width = n2[0].shape
    rows, seq, units = half // 2, 2 * half, ub.shape[1]
    ins = (sc, *n2, *blocks, w, ub)
    outs = [((seq, units), BF), ((seq, units), BF), ((seq, width), BF)]
    outs += [((half, width), BF)] * 4 + [((1, units), F32)]
    return call(
        functools.partial(mlp_kernel, rows, s), "mlp", ins,
        [SM] + [VM] * 8, outs, [],
        8 * seq * width * units, seq * units, limit=22,
    )


def pair_kernel(n, plan, pad, *refs):
    ins, out = refs[:n], refs[n]
    depth = out.shape[0]
    step = 384 if depth % 384 == 0 else depth
    for at, pairs in plan:
        for a in range(0, depth, step):
            total = None
            for l, r, first in pairs:
                right = ins[r][first : first + ins[l].shape[0], :]
                now = dg(ins[l][:, a : a + step], right, 0, 0)
                total = now if total is None else total + now
            if pad:
                fill = (-total.shape[1]) % 128
                total = jnp.concatenate([total, jnp.zeros((step, fill), F32)], 1)
            out[a : a + step, at : at + total.shape[1]] = total.astype(BF)


def weight_sums(name, depth, width, plan, pad=False, limit=23):
    ins, table, out, flops = [], {}, [], 0

    def index(x):
        if id(x) not in table:
            table[id(x)] = len(ins)
            ins.append(x)
        return table[id(x)]

    for at, pairs in plan:
        out.append((at, [(index(l), index(r), first) for l, r, first in pairs]))
        flops += sum(2 * l.shape[0] * l.shape[1] * r.shape[1] for l, r, _ in pairs)
    return call(
        functools.partial(pair_kernel, len(ins), out, pad), name, tuple(ins), [VM] * len(ins),
        [((depth, width), BF)], [], flops, limit=limit,
    )[0]


def mlp_sums_kernel(rows, n2a0, n2b0, n2a1, n2b1, gh0, gh1, go0, go1, act0, act1, out):
    depth, units = out.shape[0], act0.shape[1]
    main = units - units % 128
    step = 384 if depth % 384 == 0 else depth
    for a in range(0, depth, step):
        cut = slice(a, a + step)
        up = None
        for na, nb, gh in ((n2a0, n2b0, gh0), (n2a1, n2b1, gh1)):
            now = dg(na[:, cut], gh[0:rows, :], 0, 0) + dg(nb[:, cut], gh[rows:, :], 0, 0)
            up = now if up is None else up + now
        last = dg(go0[:, cut], act0[:, main:], 0, 0) + dg(go1[:, cut], act1[:, main:], 0, 0)
        fill = jnp.zeros((step, 128 - 2 * (units - main)), F32)
        out[cut, 0 : main + 128] = jnp.concatenate([up, last, fill], 1).astype(BF)
        out[cut, main + 128 :] = (
            dg(go0[:, cut], act0[:, 0:main], 0, 0) + dg(go1[:, cut], act1[:, 0:main], 0, 0)
        ).astype(BF)


def mlp_sums(n2s, ghs, gos, acts, packed):
    rows, width = n2s[0][0].shape
    ins = (*n2s[0], *n2s[1], *ghs, *gos, *acts)
    return call(
        functools.partial(mlp_sums_kernel, rows), "mlp_dw", ins, [VM] * 10, [((width, packed), BF)], [],
        16 * rows * width * acts[0].shape[1], limit=23,
    )[0]


def middle_kernel(rows, slot, xo, xf, chip_ref, far_ref, vec_ref, mid_ref, n2_ref):
    parts = []
    for i, ref in enumerate((xo, xf)):
        a, b = i * rows, (1 - i) * rows
        mid = ref[slot].astype(F32) + (
            chip_ref[a : a + rows, :].astype(F32) + far_ref[b : b + rows, :].astype(F32)
        ) + vec_ref[2:3, :]
        mid_ref[a : a + rows, :] = mid
        parts.append(normal(mid)[0] * vec_ref[3:4, :] + vec_ref[4:5, :])
    n2_ref[...] = jnp.concatenate(parts, 0).astype(BF)


def middle_norm(s, xo, xf, chip, far, vec):
    half, width = chip.shape
    rows = half // 2
    return call(
        functools.partial(middle_kernel, rows, s), "middle_norm", (xo, xf, chip, far, vec),
        [VM] * 5, [((half, width), F32), ((half, width), BF)], [], 20 * half * width, limit=5,
    )


def middle_back_kernel(rows, slot, sc_ref, co, cf, chip_ref, far_ref, mid_ref, vec_ref, gm_ref, gml_ref, sum_ref):
    parts = []
    for i, ref in enumerate((co, cf)):
        a, b = i * rows, (1 - i) * rows
        pos = lax.broadcasted_iota(jnp.int32, ref.shape[1:], 0) + (sc_ref[0] ^ (2 * i)) * rows
        go = jnp.where(pos < sc_ref[1], ref[slot].astype(F32), 0.0)
        grad = chip_ref[a : a + rows, :].astype(F32) + far_ref[b : b + rows, :].astype(F32)
        hat, inverse = normal(mid_ref[a : a + rows, :])
        gm = go + normal_back(hat, inverse, grad * vec_ref[3:4, :])
        parts.append(gm)
        if i == 0:
            gm_ref[...] = gm
            sum_ref[0:1, :] = jnp.sum(gm, 0, keepdims=True)
            sum_ref[1:2, :] = jnp.sum(hat * grad, 0, keepdims=True)
            sum_ref[2:3, :] = jnp.sum(grad, 0, keepdims=True)
            sum_ref[3:4, :] = jnp.sum(go, 0, keepdims=True)
    gml_ref[...] = jnp.concatenate(parts, 0).astype(BF)


def middle_back(s, sc, co, cf, chip, far, mid, vec):
    half, width = chip.shape
    rows = half // 2
    return call(
        functools.partial(middle_back_kernel, rows, s), "middle_bwd", (sc, co, cf, chip, far, mid, vec),
        [SM] + [VM] * 6,
        [((rows, width), F32), ((half, width), BF), ((4, width), F32)], [], 40 * half * width, limit=10,
    )


def input_back_kernel(rows, slot, xo, keep_ref, near_ref, far_ref, gm_ref, vec_ref, out_ref, sum_ref):
    grad = (
        keep_ref[0:rows, :].astype(F32) + near_ref[0:rows, :].astype(F32) + far_ref[...].astype(F32)
    )
    hat, inverse = normal(xo[slot].astype(F32))
    out_ref[...] = gm_ref[...] + normal_back(hat, inverse, grad * vec_ref[0:1, :])
    sum_ref[0:1, :] = jnp.sum(hat * grad, 0, keepdims=True)
    sum_ref[1:2, :] = jnp.sum(grad, 0, keepdims=True)


def input_back(s, xo, keep, near, far, gm, vec):
    rows, width = far.shape
    return call(
        functools.partial(input_back_kernel, rows, s), "input_bwd", (xo, keep, near, far, gm, vec),
        [VM] * 6, [((rows, width), F32), ((2, width), F32)], [],
        30 * rows * width, limit=5,
    )


def pack_attn_kernel(*refs):
    ins, out_ref, held, lines, sems = refs[:10], refs[10], refs[11:15], refs[15:21], refs[21]
    copies = [
        pltpu.make_async_copy(src, dst, sems.at[i]) for i, (src, dst) in enumerate(zip(ins, held + lines))
    ]
    for copy in copies:
        copy.start()
    for copy in copies:
        copy.wait()
    shard, hw = held[0].shape
    out_ref[0:shard, 0:hw] = held[3][...].astype(F32).T.astype(BF)
    for i in range(3):
        out_ref[0:shard, (i + 1) * hw : (i + 2) * hw] = held[i][...]
    rows = [ref[...].astype(F32).reshape(1, shard) for ref in lines]
    rows = jnp.concatenate(rows + [jnp.zeros((2, shard), F32)], 0)
    rows = jnp.concatenate([rows, jnp.zeros((8, 4 * hw - shard), F32)], 1)
    out_ref[shard : shard + 8, :] = rows.astype(BF)


def pack_mlp_kernel(ready, leave, u_ref, d_ref, out_ref):
    ready(0, 1)
    shard, units = u_ref.shape
    main = units - units % 128
    down = d_ref[...].astype(F32).T
    fill = jnp.zeros((shard, 128 - 2 * (units - main)), F32)
    out_ref[:, 0 : main + 128] = jnp.concatenate(
        [u_ref[...].astype(F32), down[:, main:], fill], 1
    ).astype(BF)
    out_ref[:, main + 128 :] = down[:, 0:main].astype(BF)


def place_kernel(n, cuts, idx_ref, *refs):
    sources, outs, sems = refs[:n], refs[n:-1], refs[-1]
    copies = []
    for i, src in enumerate(sources):
        for o, (a, b) in enumerate(cuts):
            dst = outs[o].at[idx_ref[i]]
            copies.append(pltpu.make_async_copy(src.at[a:b], dst, sems.at[len(copies)]))
    for c in copies:
        c.start()
    for c in copies:
        c.wait()


def place_shards(idx, sources, cuts):
    n = len(sources)
    cols = sources[0].shape[1]
    outs = [((n, b - a, cols), BF) for a, b in cuts]
    return call(
        functools.partial(place_kernel, n, cuts), "place_shards", (idx, *sources), [SM] + [HBM] * n,
        outs, [pltpu.SemaphoreType.DMA((n * len(cuts),))], 0, limit=6,
    )


def close_kernel(n, *refs):
    total = refs[0][...].astype(F32)
    for ref in refs[1:n]:
        total = total + ref[...].astype(F32)
    hw = total.shape[1] // 4
    for i in range(3):
        refs[n + i][...] = total[:, (i + 1) * hw : (i + 2) * hw]
    refs[n + 3][...] = total[:, 0:hw].T


def close_sums(parts, hw):
    rows, n = parts[0].shape[0], len(parts)
    return call(
        functools.partial(close_kernel, n), "close_sums", tuple(parts), [VM] * n,
        [((rows, hw), F32)] * 3 + [((hw, rows), F32)], [], 8 * rows * hw * n, limit=8,
    )


def after(x, *others):
    return lax.optimization_barrier((x, *others))[0]


def local(
    inputs,
    cotangent,
    lengths,
    ln1_gain,
    ln1_bias,
    q_weight,
    q_bias,
    k_weight,
    v_weight,
    v_bias,
    out_weight,
    out_bias,
    ln2_gain,
    ln2_bias,
    up_weight,
    up_bias,
    down_weight,
    down_bias,
):
    tp = lax.axis_size("tp")
    fs = lax.axis_size("fsdp")
    ti = lax.axis_index("tp")
    fi = lax.axis_index("fsdp")
    slots, rows, width = inputs.shape
    half = 2 * rows
    hw = q_weight.shape[1]
    units = up_weight.shape[1]
    shard = width // fs
    zi, yi = fi // 2, fi % 2

    def swap_tp(x, k):
        return lax.ppermute(x, "tp", [(i, i ^ k) for i in range(tp)])

    def swap_fs(x, k):
        return lax.ppermute(x, "fsdp", [(i, i ^ k) for i in range(fs)])

    def turn(x, k):
        return lax.ppermute(x, "fsdp", [(i, (i + 2 * k) % fs) for i in range(fs)])

    def gather_shards(own, cuts, beside, later):
        if fs != 8:
            whole = lax.all_gather(own, "fsdp", axis=0)
            return tuple(whole[:, a:b] for a, b in cuts), beside(own), later(own), whole
        first = lax.optimization_barrier((turn(own, 1), turn(own, 3), swap_fs(own, 1), beside(own)))
        r1, r3, o0, extra = first
        own, r1, r3, extra = lax.optimization_barrier((own, r1, r3, extra))
        second = (turn(own, 2), swap_fs(r1, 1), swap_fs(r3, 1), later(extra))
        r2, o1, o3, extra2 = lax.optimization_barrier(second)
        o2 = swap_fs(r2, 1)
        order = jnp.stack([(zi + 4 - k) % 4 for k in (0, 1, 3, 2)]) * 2
        idx = jnp.concatenate([order + yi, order + 1 - yi]).astype(jnp.int32)
        sources = [own, r1, r3, r2, o0, o1, o3, o2]
        return place_shards(idx, sources, cuts), extra, extra2, r1

    def scatter_sums(total, beside):
        if fs != 8:
            return [lax.psum_scatter(total, "fsdp", scatter_dimension=0, tiled=True)], beside
        cols = total.shape[1]
        parts = total.reshape(4, 2, shard, cols)

        def pick(k, y):
            return lax.dynamic_slice(parts, ((zi + k) % 4, y, 0, 0), (1, 1, shard, cols))[0, 0]

        first = swap_fs(jnp.stack([pick(k, 1 - yi) for k in (1, 3, 2)], 0), 1)
        mine = swap_fs(pick(0, 1 - yi), 1)
        sums = [(pick(k, yi).astype(F32) + first[j].astype(F32)).astype(BF) for j, k in enumerate((1, 3, 2))]
        *sums, beside = lax.optimization_barrier((*sums, beside))
        got = [turn(a, k) for a, k in zip(sums, (1, 3, 2))]
        return [pick(0, yi), mine, *got], beside

    def chip_sum(keep, send):
        return (keep.astype(F32) + swap_tp(send, 1).astype(F32)).astype(BF)

    def own_part(keep, send):
        near = swap_tp(send, 1)
        far = (keep[rows:].astype(F32) + near[rows:].astype(F32)).astype(BF)
        return near, swap_tp(far, 2)

    shards = (q_weight, k_weight, v_weight, out_weight)
    lines = (ln1_gain, ln1_bias, out_bias, ln2_gain, ln2_bias, down_bias)
    pack = call(
        pack_attn_kernel, "pack_attn", (*shards, *lines), [HBM] * 10, [((shard + 8, 4 * hw), BF)],
        [pltpu.VMEM(a.shape, BF) for a in shards + lines] + [pltpu.SemaphoreType.DMA((10,))], 0, limit=60,
    )[0]
    (w_attn, small), x_far, c_far, sent = gather_shards(
        pack,
        ((0, shard), (shard, shard + 8)),
        lambda _: swap_tp(inputs, 2),
        lambda x: swap_tp(after(cotangent, x), 2),
    )
    x_blocks = (inputs, x_far, swap_tp(inputs, 1), swap_tp(x_far, 1))
    c_blocks = (cotangent, c_far, swap_tp(cotangent, 1), swap_tp(c_far, 1))
    w_attn = w_attn.reshape(width, 4 * hw)
    vec = small[:, :, :shard].transpose(1, 0, 2).reshape(8, width).astype(F32)
    main = units - units % 128
    packed = 2 * main + 128
    pack = staged(
        pack_mlp_kernel, "pack_mlp", (up_weight, down_weight), ["H", "H"], [((shard, packed), BF)],
        ["V"], [], 0, limit=60
    )[0]
    w_mlp = lax.all_gather(after(pack, sent), "fsdp", axis=0, tiled=True)

    none = jnp.zeros_like(q_bias)
    shift = jnp.concatenate([none, q_bias, none, v_bias], 0).astype(F32)[None, :]
    ub = up_bias.astype(F32)[None, :]
    scalars = [jnp.stack([ti, lengths[s]]).astype(jnp.int32) for s in range(slots)]

    every = range(slots)
    fwd, chips, mids, mlps = [], [], [], []
    w_now, fars = w_attn, []
    for s in every:
        fwd.append(attn(s, scalars[s], x_blocks, vec, shift, w_now))
        keep, send = fwd[s][4:6]
        if s == 1:
            fars[0], send = lax.optimization_barrier((fars[0], send))
        chip = chip_sum(keep, send)
        if s < slots - 1:
            chip, w_now = lax.optimization_barrier((chip, w_now))
        chips.append(chip)
        fars.append(swap_tp(chip, 2))
    for s in every:
        far = fars[s]
        if s == 0:
            far, w_mlp = lax.optimization_barrier((far, w_mlp))
        mid, n2 = middle_norm(s, x_blocks[0], x_blocks[1], chips[s], far, vec)
        mids.append((mid, (n2, swap_tp(n2, 1))))
    chips = []
    w_now = w_mlp
    for s in every:
        mlps.append(mlp(s, scalars[s], mids[s][1], c_blocks, w_now, ub))
        chip = chip_sum(mlps[s][5], mlps[s][6])
        if s < slots - 1:
            chip, w_now = lax.optimization_barrier((chip, w_now))
        chips.append(chip)
    fars = [swap_tp(c, 2) for c in chips]
    acts = [m[0] for m in mlps]
    acts[0], fars[0] = lax.optimization_barrier((acts[0], fars[0]))
    g_mlp = mlp_sums([m[1] for m in mids], [m[1] for m in mlps], [m[2] for m in mlps], acts, packed)
    r_mlp = lax.psum_scatter(g_mlp, "fsdp", scatter_dimension=0, tiled=True).astype(F32)
    outs, grads_x = [], []
    wide = cols = None
    heads_out, heads_in = [], []
    mid_now = [m[0] for m in mids]
    for s in every:
        okeep, osend = mlps[s][3:5]
        gm, gml, sums = middle_back(
            s, scalars[s], c_blocks[0], c_blocks[1], chips[s], fars[s], mid_now[s], vec
        )
        gml = (gml, swap_tp(gml, 1))
        n1, qkv, mixed, lse = fwd[s][:4]
        gqkv, keep, send, col = attn_back(scalars[s], gml, w_attn, qkv, lse)
        if s < slots - 1:
            mid_now[s + 1], col = lax.optimization_barrier((mid_now[s + 1], col))
        near, far = own_part(keep, send)
        grad, sums1 = input_back(s, x_blocks[0], keep, near, far, gm, vec)
        grads_x.append(grad)
        near, far = own_part(okeep, osend)
        outs.append(
            (
                mids[s][0][:rows]
                + (okeep[:rows].astype(F32) + near[:rows].astype(F32) + far.astype(F32))
                + vec[5:6]
            ).astype(BF)
        )
        now = jnp.concatenate([sums1, sums], 0)
        wide = now if wide is None else wide + now
        cols = col if cols is None else cols + col
        heads_out += [(gml[i], mixed, i * half) for i in range(2)]
        heads_in.append((n1, gqkv, 0))
    g_attn = weight_sums("attn_dw", width, 4 * hw, [(0, heads_in), (0, heads_out)])

    unit_sums = sum(m[7] for m in mlps)
    wide = wide + swap_tp(wide, 1)
    wide = wide + swap_tp(wide, 2)
    flat = jnp.concatenate(
        [wide.reshape(-1), cols[0, hw : 2 * hw], cols[0, 3 * hw :], unit_sums[0]], 0
    )
    step = 1
    while step < fs:
        flat = flat + swap_fs(flat, step)
        step *= 2
    parts, flat = scatter_sums(g_attn, flat)
    r_up = r_mlp[:, :units]
    r_down = jnp.concatenate([r_mlp[:, main + 128 :], r_mlp[:, units : 2 * units - main]], 1).T
    parts, r_up, r_down = lax.optimization_barrier((parts, r_up, r_down))
    gq, gk, gv, go = close_sums(parts, hw)
    wide = flat[: 6 * width].reshape(6, width)
    wide = lax.dynamic_slice_in_dim(wide, fi * shard, shard, 1)
    tail = flat[6 * width :]
    return (
        jnp.stack(outs, 0),
        jnp.stack(grads_x, 0),
        wide[0],
        wide[1],
        gq,
        tail[:hw],
        gk,
        gv,
        tail[hw : 2 * hw],
        go,
        wide[2],
        wide[3],
        wide[4],
        r_up,
        tail[2 * hw :],
        r_down,
        wide[5],
    )


def solution(mesh):
    rowed = P("fsdp", "tp", None)
    wide = P("fsdp")
    cols = P("fsdp", "tp")
    turned = P("tp", "fsdp")
    part = P("tp")
    in_specs = (
        rowed, rowed, wide, wide, wide, cols, part, cols, cols, part, turned, wide,
        wide, wide, cols, part, turned, wide,
    )
    out_specs = (
        rowed, rowed, wide, wide, cols, part, cols, cols, part, turned, wide, wide, wide,
        cols, part, turned, wide,
    )
    return jax.shard_map(local, mesh=mesh, in_specs=in_specs, out_specs=out_specs, check_vma=False)
```

```python
import functools

import jax
import jax.numpy as jnp
from jax import lax
from jax.experimental import pallas as pl
from jax.experimental.pallas import tpu as pltpu
from jax.sharding import PartitionSpec as P

HD = 72
EPS = 1e-06
BF = jnp.bfloat16
F32 = jnp.float32
LOG2E = 1.4426950408889634
CHUNK = 16
VM = pl.BlockSpec(memory_space=pltpu.VMEM)
SM = pl.BlockSpec(memory_space=pltpu.SMEM)
HBM = pl.BlockSpec(memory_space=pl.ANY)


def dg(a, b, ca, cb):
    return lax.dot_general(a, b, (((ca,), (cb,)), ((), ())), preferred_element_type=F32)


def call(body, name, ins, specs, outs, scratch, flops, exps=0, limit=48):
    shapes = [jax.ShapeDtypeStruct(s, d) for s, d in outs]
    moved = sum(a.size * a.dtype.itemsize for a in ins)
    moved += sum(s.size * s.dtype.itemsize for s in shapes)
    return pl.pallas_call(
        body,
        out_shape=shapes,
        in_specs=specs,
        out_specs=[VM] * len(outs),
        scratch_shapes=scratch,
        compiler_params=pltpu.CompilerParams(vmem_limit_bytes=limit << 20),
        name=name,
        cost_estimate=pl.CostEstimate(
            flops=int(flops), bytes_accessed=int(moved), transcendentals=int(exps)
        ),
    )(*ins)


def staged(body, name, ins, modes, outs, out_modes, scratch, flops, exps=0, limit=44):
    shapes = [jax.ShapeDtypeStruct(s, d) for s, d in outs]
    kinds = {"S": SM, "V": VM}
    buffers, moves = [], 0
    for x, m in zip(ins, modes):
        if m not in ("S", "V", "A"):
            buffers.append(pltpu.VMEM(x.shape if m == "H" else x.shape[1:], x.dtype))
            moves += 1
    for (shape, kind), m in zip(outs, out_modes):
        if m == "H":
            buffers.append(pltpu.VMEM(shape, kind))
            moves += 4
    n_in, n_out, n_own = len(ins), len(outs), len(scratch)

    def kernel(*refs):
        in_refs, out_refs = refs[:n_in], refs[n_in : n_in + n_out]
        own = refs[n_in + n_out : n_in + n_out + n_own]
        spare = list(refs[n_in + n_out + n_own : -1])
        sems = refs[-1]
        used = []

        def copy(src, dst):
            c = pltpu.make_async_copy(src, dst, sems.at[len(used)])
            c.start()
            used.append(c)
            return c

        views, arriving, out_views, leaving = [], {}, [], []
        for i, (ref, m) in enumerate(zip(in_refs, modes)):
            if m in ("S", "V", "A"):
                views.append(ref)
            else:
                buf = spare.pop(0)
                arriving[i] = copy(ref if m == "H" else ref.at[m], buf)
                views.append(buf)
        for ref, m in zip(out_refs, out_modes):
            out_views.append(spare.pop(0) if m == "H" else ref)

        def ready(*which):
            for i in which:
                if i in arriving:
                    arriving.pop(i).wait()

        def leave(o, a, b):
            if out_modes[o] == "H":
                leaving.append(copy(out_views[o].at[a:b], out_refs[o].at[a:b]))

        body(ready, leave, *views, *out_views, *own)
        for c in leaving:
            c.wait()

    moved = sum(a.size * a.dtype.itemsize for a in ins) + sum(
        s.size * s.dtype.itemsize for s in shapes
    )
    return pl.pallas_call(
        kernel,
        out_shape=shapes,
        in_specs=[kinds.get(m, HBM) for m in modes],
        out_specs=[HBM if m == "H" else VM for m in out_modes],
        scratch_shapes=list(scratch) + buffers + [pltpu.SemaphoreType.DMA((max(moves, 1),))],
        compiler_params=pltpu.CompilerParams(vmem_limit_bytes=limit << 20),
        name=name,
        cost_estimate=pl.CostEstimate(
            flops=int(flops), bytes_accessed=int(moved), transcendentals=int(exps)
        ),
    )(*ins)


def normal(x):
    average = jnp.mean(x, -1, keepdims=True)
    center = x - average
    variance = jnp.mean(center * center, -1, keepdims=True)
    inverse = lax.rsqrt(variance + EPS)
    return center * inverse, inverse


def normal_back(hat, inverse, scaled):
    first = jnp.mean(scaled, -1, keepdims=True)
    second = jnp.mean(scaled * hat, -1, keepdims=True)
    return inverse * (scaled - first - hat * second)


def positions(sc_ref, rows, shape, dim):
    r = lax.broadcasted_iota(jnp.int32, shape, dim)
    ti = sc_ref[0]
    p0, p2, p1, p3 = ((ti ^ j) * rows for j in (0, 2, 1, 3))
    return jnp.where(
        r < 2 * rows,
        jnp.where(r < rows, r + p0, r + (p2 - rows)),
        jnp.where(r < 3 * rows, r + (p1 - 2 * rows), r + (p3 - 3 * rows)),
    )


def attn_kernel(heads, rows, slot, sc_ref, xo, xf, xno, xnf, vec_ref, shift_ref, w_ref,
                n1_ref, qkv_ref, mixed_ref, lse_ref, keep_ref, send_ref, s_ref, p_ref):
    seq = 4 * rows
    half = 2 * rows
    hw = heads * HD
    c = LOG2E * HD**-0.5
    gain, bias = vec_ref[0:1, :], vec_ref[1:2, :]
    for i, pair in enumerate(((xo, xf), (xno, xnf))):
        parts = [normal(ref[slot].astype(F32))[0] * gain + bias for ref in pair]
        n1 = jnp.concatenate(parts, 0).astype(BF)
        n1_ref[i * half : (i + 1) * half, :] = n1
        qkv_ref[i * half : (i + 1) * half, :] = (dg(n1, w_ref[...], 1, 0) + shift_ref[...]).astype(BF)
    lane = lax.broadcasted_iota(jnp.int32, (seq, 128), 1)
    pos = positions(sc_ref, rows, (seq, 128), 0)
    mask = jnp.where((lane == HD) & (pos >= sc_ref[1]), -1e30, 0.0).astype(BF)
    one = jnp.where(lane == HD, 1.0, 0.0).astype(BF)
    for h in range(heads):
        a = hw + HD * h
        qx = jnp.where(lane < HD, qkv_ref[:, a : a + 128], one)
        kx = jnp.where(lane < HD, qkv_ref[:, hw + a : hw + a + 128], mask)
        v = qkv_ref[:, 2 * hw + a : 2 * hw + a + HD]
        sl = h % 2
        s_ref[sl] = dg(kx, qx, 1, 1)
        m = s_ref[sl, 0:CHUNK, :]
        for r in range(CHUNK, seq, CHUNK):
            m = jnp.maximum(m, s_ref[sl, r : r + CHUNK, :])
        m = jnp.max(m, 0, keepdims=True) * c
        total = jnp.zeros((CHUNK, seq), F32)
        for r in range(0, seq, CHUNK):
            p = jnp.exp2(s_ref[sl, r : r + CHUNK, :] * c - m)
            total = total + p
            p_ref[sl, r : r + CHUNK, :] = p.astype(BF)
        total = jnp.sum(total, 0, keepdims=True)
        lse_ref[h : h + 1, :] = m + jnp.log2(total)
        mixed = dg(v, p_ref[sl], 0, 0) * (1.0 / total)
        mixed_ref[:, HD * h : HD * h + HD] = mixed.T.astype(BF)
    for i, ref in enumerate((keep_ref, send_ref)):
        ref[...] = dg(mixed_ref[i * half : (i + 1) * half, :], w_ref[:, 0:hw], 1, 1).astype(BF)


def attn(s, sc, blocks, vec, shift, w):
    rows, width = blocks[0].shape[1:]
    seq, hw = 4 * rows, w.shape[1] // 4
    heads = hw // HD
    ins = (sc, *blocks, vec, shift, w)
    outs = [((seq, width), BF), ((seq, 4 * hw), BF), ((seq, hw), BF), ((8, seq), F32)]
    outs += [((2 * rows, width), BF)] * 2
    return call(
        functools.partial(attn_kernel, heads, rows, s), "attn_fwd", ins,
        [SM] + [VM] * 7, outs,
        [pltpu.VMEM((2, seq, seq), F32), pltpu.VMEM((2, seq, seq), BF)],
        2 * seq * width * 5 * hw + 16 * seq * seq * 128 * heads, heads * seq * seq, limit=20,
    )


def attn_back_kernel(heads, rows, sc_ref, ga_ref, gb_ref, w_ref, qkv_ref, lse_ref,
                     gq_ref, keep_ref, send_ref, col_ref, s_ref, g_ref, p_ref, d_ref, gm_ref):
    seq = 4 * rows
    half = 2 * rows
    hw = heads * HD
    scale = HD**-0.5
    c = LOG2E * scale
    for i, ref in enumerate((ga_ref, gb_ref)):
        gm_ref[i * half : (i + 1) * half, :] = dg(ref[...], w_ref[:, 0:hw], 1, 0).astype(BF)
    lane = lax.broadcasted_iota(jnp.int32, (seq, 128), 1)
    pos = positions(sc_ref, rows, (seq, 128), 0)
    mask = jnp.where((lane == HD) & (pos >= sc_ref[1]), -1e30, 0.0).astype(BF)
    one = jnp.where(lane == HD, 1.0, 0.0).astype(BF)
    gq_ref[:, 0:hw] = jnp.zeros((seq, hw), BF)
    for h in range(heads):
        a = hw + HD * h
        qx = jnp.where(lane < HD, qkv_ref[:, a : a + 128], one)
        kx = jnp.where(lane < HD, qkv_ref[:, hw + a : hw + a + 128], mask)
        q = qkv_ref[:, a : a + HD]
        k = qkv_ref[:, hw + a : hw + a + HD]
        v = qkv_ref[:, 2 * hw + a : 2 * hw + a + HD]
        g = gm_ref[:, HD * h : HD * h + HD]
        sl = h % 2
        s_ref[sl] = dg(kx, qx, 1, 1)
        g_ref[sl] = dg(v, g, 1, 1)
        lse = lse_ref[h : h + 1, :]
        inner = jnp.zeros((CHUNK, seq), F32)
        for r in range(0, seq, CHUNK):
            p = jnp.exp2(s_ref[sl, r : r + CHUNK, :] * c - lse)
            s_ref[sl, r : r + CHUNK, :] = p
            p_ref[sl, r : r + CHUNK, :] = p.astype(BF)
            inner = inner + p * g_ref[sl, r : r + CHUNK, :]
        inner = jnp.sum(inner, 0, keepdims=True)
        for r in range(0, seq, CHUNK):
            d_ref[sl, r : r + CHUNK, :] = (
                s_ref[sl, r : r + CHUNK, :] * (g_ref[sl, r : r + CHUNK, :] - inner)
            ).astype(BF)
        gq_ref[:, a : a + HD] = (dg(k, d_ref[sl], 0, 0) * scale).T.astype(BF)
        gq_ref[:, hw + a : hw + a + HD] = (dg(d_ref[sl], q, 1, 0) * scale).astype(BF)
        gq_ref[:, 2 * hw + a : 2 * hw + a + HD] = dg(p_ref[sl], g, 1, 0).astype(BF)
    col = None
    for i, ref in enumerate((keep_ref, send_ref)):
        part = gq_ref[i * half : (i + 1) * half, :]
        ref[...] = dg(part, w_ref[...], 1, 1).astype(BF)
        now = jnp.sum(part.astype(F32), 0, keepdims=True)
        col = now if col is None else col + now
    col_ref[...] = col


def attn_back(sc, gml, w, qkv, lse):
    half, width = gml[0].shape
    seq, hw = 2 * half, w.shape[1] // 4
    heads = hw // HD
    ins = (sc, *gml, w, qkv, lse)
    outs = [((seq, 4 * hw), BF), ((half, width), BF), ((half, width), BF), ((1, 4 * hw), F32)]
    return call(
        functools.partial(attn_back_kernel, heads, half // 2), "attn_bwd", ins,
        [SM] + [VM] * 5, outs,
        [pltpu.VMEM((2, seq, seq), F32)] * 2 + [pltpu.VMEM((2, seq, seq), BF)] * 2
        + [pltpu.VMEM((seq, hw), BF)],
        2 * seq * width * 5 * hw + 24 * seq * seq * 128 * heads, heads * seq * seq, limit=30,
    )


def mlp_kernel(rows, slot, sc_ref, na_ref, nb_ref, co, cf, cno, cnf, w_ref, ub_ref,
               act_ref, gh_ref, go_ref, okeep_ref, osend_ref, gkeep_ref, gsend_ref, us_ref):
    half = 2 * rows
    c0 = 0.7978845608028654
    limit = sc_ref[1]
    us = None
    units = ub_ref.shape[1]
    main = units - units % 128
    wu_ref = w_ref.at[:, 0:units]
    wa_ref, wb_ref = w_ref.at[:, main + 128 :], w_ref.at[:, units : 2 * units - main]
    for i, (n_ref, pair, o_ref, g_ref) in enumerate((
        (na_ref, (co, cf), okeep_ref, gkeep_ref),
        (nb_ref, (cno, cnf), osend_ref, gsend_ref),
    )):
        parts = []
        for j, ref in enumerate(pair):
            start = (sc_ref[0] ^ ((0, 2, 1, 3)[2 * i + j])) * rows
            pos = lax.broadcasted_iota(jnp.int32, ref.shape[1:], 0) + start
            parts.append(jnp.where(pos < limit, ref[slot].astype(F32), 0.0))
        go = jnp.concatenate(parts, 0).astype(BF)
        go_ref[i * half : (i + 1) * half, :] = go
        hidden = dg(n_ref[...], wu_ref[...], 1, 0) + ub_ref[...]
        square = hidden * hidden
        t = jnp.tanh(hidden * (c0 + (c0 * 0.044715) * square))
        act = (0.5 * hidden * (1.0 + t)).astype(BF)
        slope = 0.5 * (1.0 + t) + hidden * (1.0 - t * t) * (0.5 * c0 + (1.5 * c0 * 0.044715) * square)
        act_ref[i * half : (i + 1) * half, :] = act
        o_ref[...] = (
            dg(act[:, 0:main], wa_ref[...], 1, 1) + dg(act[:, main:], wb_ref[...], 1, 1)
        ).astype(BF)
        grad = jnp.concatenate([dg(go, wa_ref[...], 1, 0), dg(go, wb_ref[...], 1, 0)], 1)
        gh = (grad * slope).astype(BF)
        gh_ref[i * half : (i + 1) * half, :] = gh
        g_ref[...] = dg(gh, wu_ref[...], 1, 1).astype(BF)
        now = jnp.sum(gh.astype(F32), 0, keepdims=True)
        us = now if us is None else us + now
    us_ref[...] = us


def mlp(s, sc, n2, blocks, w, ub):
    half, width = n2[0].shape
    rows, seq, units = half // 2, 2 * half, ub.shape[1]
    ins = (sc, *n2, *blocks, w, ub)
    outs = [((seq, units), BF), ((seq, units), BF), ((seq, width), BF)]
    outs += [((half, width), BF)] * 4 + [((1, units), F32)]
    return call(
        functools.partial(mlp_kernel, rows, s), "mlp", ins,
        [SM] + [VM] * 8, outs, [],
        8 * seq * width * units, seq * units, limit=22,
    )


def pair_kernel(n, plan, pad, *refs):
    ins, out = refs[:n], refs[n]
    depth = out.shape[0]
    step = 384 if depth % 384 == 0 else depth
    for at, pairs in plan:
        for a in range(0, depth, step):
            total = None
            for l, r, first in pairs:
                right = ins[r][first : first + ins[l].shape[0], :]
                now = dg(ins[l][:, a : a + step], right, 0, 0)
                total = now if total is None else total + now
            if pad:
                fill = (-total.shape[1]) % 128
                total = jnp.concatenate([total, jnp.zeros((step, fill), F32)], 1)
            out[a : a + step, at : at + total.shape[1]] = total.astype(BF)


def weight_sums(name, depth, width, plan, pad=False, limit=23):
    ins, table, out, flops = [], {}, [], 0

    def index(x):
        if id(x) not in table:
            table[id(x)] = len(ins)
            ins.append(x)
        return table[id(x)]

    for at, pairs in plan:
        out.append((at, [(index(l), index(r), first) for l, r, first in pairs]))
        flops += sum(2 * l.shape[0] * l.shape[1] * r.shape[1] for l, r, _ in pairs)
    return call(
        functools.partial(pair_kernel, len(ins), out, pad), name, tuple(ins), [VM] * len(ins),
        [((depth, width), BF)], [], flops, limit=limit,
    )[0]


def mlp_sums_kernel(rows, n2a0, n2b0, n2a1, n2b1, gh0, gh1, go0, go1, act0, act1, out):
    depth, units = out.shape[0], act0.shape[1]
    main = units - units % 128
    step = 384 if depth % 384 == 0 else depth
    for a in range(0, depth, step):
        cut = slice(a, a + step)
        up = None
        for na, nb, gh in ((n2a0, n2b0, gh0), (n2a1, n2b1, gh1)):
            now = dg(na[:, cut], gh[0:rows, :], 0, 0) + dg(nb[:, cut], gh[rows:, :], 0, 0)
            up = now if up is None else up + now
        last = dg(go0[:, cut], act0[:, main:], 0, 0) + dg(go1[:, cut], act1[:, main:], 0, 0)
        fill = jnp.zeros((step, 128 - 2 * (units - main)), F32)
        out[cut, 0 : main + 128] = jnp.concatenate([up, last, fill], 1).astype(BF)
        out[cut, main + 128 :] = (
            dg(go0[:, cut], act0[:, 0:main], 0, 0) + dg(go1[:, cut], act1[:, 0:main], 0, 0)
        ).astype(BF)


def mlp_sums(n2s, ghs, gos, acts, packed):
    rows, width = n2s[0][0].shape
    ins = (*n2s[0], *n2s[1], *ghs, *gos, *acts)
    return call(
        functools.partial(mlp_sums_kernel, rows), "mlp_dw", ins, [VM] * 10, [((width, packed), BF)], [],
        16 * rows * width * acts[0].shape[1], limit=23,
    )[0]


def middle_kernel(rows, slot, xo, xf, chip_ref, far_ref, vec_ref, mid_ref, n2_ref):
    parts = []
    for i, ref in enumerate((xo, xf)):
        a, b = i * rows, (1 - i) * rows
        mid = ref[slot].astype(F32) + (
            chip_ref[a : a + rows, :].astype(F32) + far_ref[b : b + rows, :].astype(F32)
        ) + vec_ref[2:3, :]
        mid_ref[a : a + rows, :] = mid
        parts.append(normal(mid)[0] * vec_ref[3:4, :] + vec_ref[4:5, :])
    n2_ref[...] = jnp.concatenate(parts, 0).astype(BF)


def middle_norm(s, xo, xf, chip, far, vec):
    half, width = chip.shape
    rows = half // 2
    return call(
        functools.partial(middle_kernel, rows, s), "middle_norm", (xo, xf, chip, far, vec),
        [VM] * 5, [((half, width), F32), ((half, width), BF)], [], 20 * half * width, limit=5,
    )


def middle_back_kernel(rows, slot, sc_ref, co, cf, chip_ref, far_ref, mid_ref, vec_ref, gm_ref, gml_ref, sum_ref):
    parts = []
    for i, ref in enumerate((co, cf)):
        a, b = i * rows, (1 - i) * rows
        pos = lax.broadcasted_iota(jnp.int32, ref.shape[1:], 0) + (sc_ref[0] ^ (2 * i)) * rows
        go = jnp.where(pos < sc_ref[1], ref[slot].astype(F32), 0.0)
        grad = chip_ref[a : a + rows, :].astype(F32) + far_ref[b : b + rows, :].astype(F32)
        hat, inverse = normal(mid_ref[a : a + rows, :])
        gm = go + normal_back(hat, inverse, grad * vec_ref[3:4, :])
        parts.append(gm)
        if i == 0:
            gm_ref[...] = gm
            sum_ref[0:1, :] = jnp.sum(gm, 0, keepdims=True)
            sum_ref[1:2, :] = jnp.sum(hat * grad, 0, keepdims=True)
            sum_ref[2:3, :] = jnp.sum(grad, 0, keepdims=True)
            sum_ref[3:4, :] = jnp.sum(go, 0, keepdims=True)
    gml_ref[...] = jnp.concatenate(parts, 0).astype(BF)


def middle_back(s, sc, co, cf, chip, far, mid, vec):
    half, width = chip.shape
    rows = half // 2
    return call(
        functools.partial(middle_back_kernel, rows, s), "middle_bwd", (sc, co, cf, chip, far, mid, vec),
        [SM] + [VM] * 6,
        [((rows, width), F32), ((half, width), BF), ((4, width), F32)], [], 40 * half * width, limit=10,
    )


def input_back_kernel(rows, slot, xo, keep_ref, near_ref, far_ref, gm_ref, vec_ref, out_ref, sum_ref):
    grad = (
        keep_ref[0:rows, :].astype(F32) + near_ref[0:rows, :].astype(F32) + far_ref[...].astype(F32)
    )
    hat, inverse = normal(xo[slot].astype(F32))
    out_ref[...] = gm_ref[...] + normal_back(hat, inverse, grad * vec_ref[0:1, :])
    sum_ref[0:1, :] = jnp.sum(hat * grad, 0, keepdims=True)
    sum_ref[1:2, :] = jnp.sum(grad, 0, keepdims=True)


def input_back(s, xo, keep, near, far, gm, vec):
    rows, width = far.shape
    return call(
        functools.partial(input_back_kernel, rows, s), "input_bwd", (xo, keep, near, far, gm, vec),
        [VM] * 6, [((rows, width), F32), ((2, width), F32)], [],
        30 * rows * width, limit=5,
    )


def pack_attn_kernel(*refs):
    ins, out_ref, held, lines, sems = refs[:10], refs[10], refs[11:15], refs[15:21], refs[21]
    copies = [
        pltpu.make_async_copy(src, dst, sems.at[i]) for i, (src, dst) in enumerate(zip(ins, held + lines))
    ]
    for copy in copies:
        copy.start()
    for copy in copies:
        copy.wait()
    shard, hw = held[0].shape
    out_ref[0:shard, 0:hw] = held[3][...].astype(F32).T.astype(BF)
    for i in range(3):
        out_ref[0:shard, (i + 1) * hw : (i + 2) * hw] = held[i][...]
    rows = [ref[...].astype(F32).reshape(1, shard) for ref in lines]
    rows = jnp.concatenate(rows + [jnp.zeros((2, shard), F32)], 0)
    rows = jnp.concatenate([rows, jnp.zeros((8, 4 * hw - shard), F32)], 1)
    out_ref[shard : shard + 8, :] = rows.astype(BF)


def pack_mlp_kernel(ready, leave, u_ref, d_ref, out_ref):
    ready(0, 1)
    shard, units = u_ref.shape
    main = units - units % 128
    down = d_ref[...].astype(F32).T
    fill = jnp.zeros((shard, 128 - 2 * (units - main)), F32)
    out_ref[:, 0 : main + 128] = jnp.concatenate(
        [u_ref[...].astype(F32), down[:, main:], fill], 1
    ).astype(BF)
    out_ref[:, main + 128 :] = down[:, 0:main].astype(BF)


def place_kernel(n, cuts, idx_ref, *refs):
    sources, outs, sems = refs[:n], refs[n:-1], refs[-1]
    copies = []
    for i, src in enumerate(sources):
        for o, (a, b) in enumerate(cuts):
            dst = outs[o].at[idx_ref[i]]
            copies.append(pltpu.make_async_copy(src.at[a:b], dst, sems.at[len(copies)]))
    for c in copies:
        c.start()
    for c in copies:
        c.wait()


def place_shards(idx, sources, cuts):
    n = len(sources)
    cols = sources[0].shape[1]
    outs = [((n, b - a, cols), BF) for a, b in cuts]
    return call(
        functools.partial(place_kernel, n, cuts), "place_shards", (idx, *sources), [SM] + [HBM] * n,
        outs, [pltpu.SemaphoreType.DMA((n * len(cuts),))], 0, limit=6,
    )


def close_kernel(n, *refs):
    total = refs[0][...].astype(F32)
    for ref in refs[1:n]:
        total = total + ref[...].astype(F32)
    hw = total.shape[1] // 4
    for i in range(3):
        refs[n + i][...] = total[:, (i + 1) * hw : (i + 2) * hw]
    refs[n + 3][...] = total[:, 0:hw].T


def close_sums(parts, hw):
    rows, n = parts[0].shape[0], len(parts)
    return call(
        functools.partial(close_kernel, n), "close_sums", tuple(parts), [VM] * n,
        [((rows, hw), F32)] * 3 + [((hw, rows), F32)], [], 8 * rows * hw * n, limit=8,
    )


def after(x, *others):
    return lax.optimization_barrier((x, *others))[0]


def local(
    inputs,
    cotangent,
    lengths,
    ln1_gain,
    ln1_bias,
    q_weight,
    q_bias,
    k_weight,
    v_weight,
    v_bias,
    out_weight,
    out_bias,
    ln2_gain,
    ln2_bias,
    up_weight,
    up_bias,
    down_weight,
    down_bias,
):
    tp = lax.axis_size("tp")
    fs = lax.axis_size("fsdp")
    ti = lax.axis_index("tp")
    fi = lax.axis_index("fsdp")
    slots, rows, width = inputs.shape
    half = 2 * rows
    hw = q_weight.shape[1]
    units = up_weight.shape[1]
    shard = width // fs
    zi, yi = fi // 2, fi % 2

    def swap_tp(x, k):
        return lax.ppermute(x, "tp", [(i, i ^ k) for i in range(tp)])

    def swap_fs(x, k):
        return lax.ppermute(x, "fsdp", [(i, i ^ k) for i in range(fs)])

    def turn(x, k):
        return lax.ppermute(x, "fsdp", [(i, (i + 2 * k) % fs) for i in range(fs)])

    def gather_shards(own, cuts, beside, later):
        if fs != 8:
            whole = lax.all_gather(own, "fsdp", axis=0)
            return tuple(whole[:, a:b] for a, b in cuts), beside(own), later(own), whole
        first = lax.optimization_barrier((turn(own, 1), turn(own, 3), swap_fs(own, 1), beside(own)))
        r1, r3, o0, extra = first
        own, r1, r3, extra = lax.optimization_barrier((own, r1, r3, extra))
        second = (turn(own, 2), swap_fs(r1, 1), swap_fs(r3, 1), later(extra))
        r2, o1, o3, extra2 = lax.optimization_barrier(second)
        o2 = swap_fs(r2, 1)
        order = jnp.stack([(zi + 4 - k) % 4 for k in (0, 1, 3, 2)]) * 2
        idx = jnp.concatenate([order + yi, order + 1 - yi]).astype(jnp.int32)
        sources = [own, r1, r3, r2, o0, o1, o3, o2]
        return place_shards(idx, sources, cuts), extra, extra2, r1

    def scatter_sums(total, beside):
        if fs != 8:
            return [lax.psum_scatter(total, "fsdp", scatter_dimension=0, tiled=True)], beside
        cols = total.shape[1]
        parts = total.reshape(4, 2, shard, cols)

        def pick(k, y):
            return lax.dynamic_slice(parts, ((zi + k) % 4, y, 0, 0), (1, 1, shard, cols))[0, 0]

        first = swap_fs(jnp.stack([pick(k, 1 - yi) for k in (1, 3, 2)], 0), 1)
        mine = swap_fs(pick(0, 1 - yi), 1)
        sums = [(pick(k, yi).astype(F32) + first[j].astype(F32)).astype(BF) for j, k in enumerate((1, 3, 2))]
        *sums, beside = lax.optimization_barrier((*sums, beside))
        got = [turn(a, k) for a, k in zip(sums, (1, 3, 2))]
        return [pick(0, yi), mine, *got], beside

    def chip_sum(keep, send):
        return (keep.astype(F32) + swap_tp(send, 1).astype(F32)).astype(BF)

    def own_part(keep, send):
        near = swap_tp(send, 1)
        far = (keep[rows:].astype(F32) + near[rows:].astype(F32)).astype(BF)
        return near, swap_tp(far, 2)

    shards = (q_weight, k_weight, v_weight, out_weight)
    lines = (ln1_gain, ln1_bias, out_bias, ln2_gain, ln2_bias, down_bias)
    pack = call(
        pack_attn_kernel, "pack_attn", (*shards, *lines), [HBM] * 10, [((shard + 8, 4 * hw), BF)],
        [pltpu.VMEM(a.shape, BF) for a in shards + lines] + [pltpu.SemaphoreType.DMA((10,))], 0, limit=60,
    )[0]
    (w_attn, small), x_far, c_far, sent = gather_shards(
        pack,
        ((0, shard), (shard, shard + 8)),
        lambda _: swap_tp(inputs, 2),
        lambda x: swap_tp(after(cotangent, x), 2),
    )
    x_blocks = (inputs, x_far, swap_tp(inputs, 1), swap_tp(x_far, 1))
    c_blocks = (cotangent, c_far, swap_tp(cotangent, 1), swap_tp(c_far, 1))
    w_attn = w_attn.reshape(width, 4 * hw)
    vec = small[:, :, :shard].transpose(1, 0, 2).reshape(8, width).astype(F32)
    main = units - units % 128
    packed = 2 * main + 128
    pack = staged(
        pack_mlp_kernel, "pack_mlp", (up_weight, down_weight), ["H", "H"], [((shard, packed), BF)],
        ["V"], [], 0, limit=60
    )[0]
    w_mlp = lax.all_gather(after(pack, sent), "fsdp", axis=0, tiled=True)

    none = jnp.zeros_like(q_bias)
    shift = jnp.concatenate([none, q_bias, none, v_bias], 0).astype(F32)[None, :]
    ub = up_bias.astype(F32)[None, :]
    scalars = [jnp.stack([ti, lengths[s]]).astype(jnp.int32) for s in range(slots)]

    every = range(slots)
    fwd, chips, mids, mlps = [], [], [], []
    w_now, fars = w_attn, []
    for s in every:
        fwd.append(attn(s, scalars[s], x_blocks, vec, shift, w_now))
        keep, send = fwd[s][4:6]
        if s == 1:
            fars[0], send = lax.optimization_barrier((fars[0], send))
        chip = chip_sum(keep, send)
        if s < slots - 1:
            chip, w_now = lax.optimization_barrier((chip, w_now))
        chips.append(chip)
        fars.append(swap_tp(chip, 2))
    for s in every:
        far = fars[s]
        if s == 0:
            far, w_mlp = lax.optimization_barrier((far, w_mlp))
        mid, n2 = middle_norm(s, x_blocks[0], x_blocks[1], chips[s], far, vec)
        mids.append((mid, (n2, swap_tp(n2, 1))))
    chips = []
    w_now = w_mlp
    for s in every:
        mlps.append(mlp(s, scalars[s], mids[s][1], c_blocks, w_now, ub))
        chip = chip_sum(mlps[s][5], mlps[s][6])
        if s < slots - 1:
            chip, w_now = lax.optimization_barrier((chip, w_now))
        chips.append(chip)
    fars = [swap_tp(c, 2) for c in chips]
    acts = [m[0] for m in mlps]
    acts[0], fars[0] = lax.optimization_barrier((acts[0], fars[0]))
    g_mlp = mlp_sums([m[1] for m in mids], [m[1] for m in mlps], [m[2] for m in mlps], acts, packed)
    r_mlp = lax.psum_scatter(g_mlp, "fsdp", scatter_dimension=0, tiled=True).astype(F32)
    outs, grads_x = [], []
    wide = cols = None
    heads_out, heads_in = [], []
    mid_now = [m[0] for m in mids]
    for s in every:
        okeep, osend = mlps[s][3:5]
        gm, gml, sums = middle_back(
            s, scalars[s], c_blocks[0], c_blocks[1], chips[s], fars[s], mid_now[s], vec
        )
        gml = (gml, swap_tp(gml, 1))
        n1, qkv, mixed, lse = fwd[s][:4]
        gqkv, keep, send, col = attn_back(scalars[s], gml, w_attn, qkv, lse)
        if s < slots - 1:
            mid_now[s + 1], col = lax.optimization_barrier((mid_now[s + 1], col))
        near, far = own_part(keep, send)
        grad, sums1 = input_back(s, x_blocks[0], keep, near, far, gm, vec)
        grads_x.append(grad)
        near, far = own_part(okeep, osend)
        outs.append(
            (
                mids[s][0][:rows]
                + (okeep[:rows].astype(F32) + near[:rows].astype(F32) + far.astype(F32))
                + vec[5:6]
            ).astype(BF)
        )
        now = jnp.concatenate([sums1, sums], 0)
        wide = now if wide is None else wide + now
        cols = col if cols is None else cols + col
        heads_out += [(gml[i], mixed, i * half) for i in range(2)]
        heads_in.append((n1, gqkv, 0))
    g_attn = weight_sums("attn_dw", width, 4 * hw, [(0, heads_in), (0, heads_out)])

    unit_sums = sum(m[7] for m in mlps)
    wide = wide + swap_tp(wide, 1)
    wide = wide + swap_tp(wide, 2)
    flat = jnp.concatenate(
        [wide.reshape(-1), cols[0, hw : 2 * hw], cols[0, 3 * hw :], unit_sums[0]], 0
    )
    step = fs // 2
    while step:
        flat = flat + swap_fs(flat, step)
        step //= 2
    parts, flat = scatter_sums(g_attn, flat)
    r_up = r_mlp[:, :units]
    r_down = jnp.concatenate([r_mlp[:, main + 128 :], r_mlp[:, units : 2 * units - main]], 1).T
    parts, r_up, r_down = lax.optimization_barrier((parts, r_up, r_down))
    gq, gk, gv, go = close_sums(parts, hw)
    wide = flat[: 6 * width].reshape(6, width)
    wide = lax.dynamic_slice_in_dim(wide, fi * shard, shard, 1)
    tail = flat[6 * width :]
    return (
        jnp.stack(outs, 0),
        jnp.stack(grads_x, 0),
        wide[0],
        wide[1],
        gq,
        tail[:hw],
        gk,
        gv,
        tail[hw : 2 * hw],
        go,
        wide[2],
        wide[3],
        wide[4],
        r_up,
        tail[2 * hw :],
        r_down,
        wide[5],
    )


def solution(mesh):
    rowed = P("fsdp", "tp", None)
    wide = P("fsdp")
    cols = P("fsdp", "tp")
    turned = P("tp", "fsdp")
    part = P("tp")
    in_specs = (
        rowed, rowed, wide, wide, wide, cols, part, cols, cols, part, turned, wide,
        wide, wide, cols, part, turned, wide,
    )
    out_specs = (
        rowed, rowed, wide, wide, cols, part, cols, cols, part, turned, wide, wide, wide,
        cols, part, turned, wide,
    )
    return jax.shard_map(local, mesh=mesh, in_specs=in_specs, out_specs=out_specs, check_vma=False)
```
